256 devices in a mesh: height: 8 (over x, core), dom: 32 (over z, y).
Axes of the slice: x: 4, y: 4, z: 8, core: 2. Of those that a mesh axis runs over, the one named last changes fastest.
Arguments:
- modes_now: float32 [64, 256, 4096], P('height', 'dom'), may hold values from -6 to 6
- modes_prev: float32 [64, 256, 4096], P('height', 'dom'), may hold values from -6 to 6
- partition_boxes: int32 [256, 2], P('dom'), may hold values from 16 to 64, as said below
- face_table: int32 [1024, 8], P('dom'), may hold values from 0 to 64, as said below
Outputs:
- new_modes: float32 [64, 256, 4096], P('height', 'dom')
- pressure: float32 [64, 256, 4096], P('height', 'dom')
The draws below stay inside these ranges and needn't reach their ends.
Inputs may be any that keep to these rules, and one draw needn't show every extreme that they name: `partition_boxes`: column 0 is a partition's extent along x, column 1 along y. `face_table`: row r belongs to dom index r // 32. Columns: 0 the local number of the source partition on that index, 1 its side (0 low x, 1 high x, 2 low y, 3 high y), 2 the first cell of the face along that side, 3 the face's length in cells (0 marks an unused row), 4 the dom index holding the target partition, 5 the target's local number, 6 its side, 7 the first cell along it. Sides 0 and 1 run along y, sides 2 and 3 along x; start plus length never passes either side's extent. Among the rows of one dom index at most 2 name the same dom index in column 4, and that many is reached in every draw.
All inputs are finite; a program needn't handle non-finite values.
Results may differ from the reference program's by a relative error of at most 0.0002.
Values sent between devices are 32-bit elements; how exact they have to be, the bound alone decides.
No kernel may reach another device: no remote copies, remote signals or barrier semaphores. Data moves between devices by JAX's collectives and lax.ppermute only.
A program may use at most 64 MiB of HBM per device.

```python
import jax
import jax.numpy as jnp
from jax import lax

B = 64
NZ = 64
PDEV = 8
FDEV = 32
PARTS_SIZE = 256
N_DOM = 32


def layout_tables(key):
    extents = jax.random.randint(jax.random.fold_in(key, 101), (N_DOM * PDEV, 2), B // 4, B + 1)
    pair_most = max(2, FDEV // N_DOM)
    groups = FDEV // pair_most
    order_key = jax.random.fold_in(key, 202)
    sources = jnp.arange(N_DOM, dtype=jnp.int32)

    def shuffled(source):
        return jax.random.permutation(jax.random.fold_in(order_key, source), N_DOM).astype(jnp.int32)
    offsets = jax.vmap(shuffled)(sources)[:, :groups]
    slot_ids = jnp.arange(FDEV, dtype=jnp.int32)
    group_of = slot_ids // pair_most
    targets = (sources[:, None] + offsets[:, group_of]) % N_DOM
    live_count = jax.random.randint(jax.random.fold_in(key, 303), (N_DOM, groups), 1, pair_most + 1)
    live_count = live_count.at[:, 0].set(pair_most)
    alive = (slot_ids % pair_most)[None, :] < live_count[:, group_of]
    grid_shape = (N_DOM, FDEV)
    src_part = jax.random.randint(jax.random.fold_in(key, 404), grid_shape, 0, PDEV)
    src_side = jax.random.randint(jax.random.fold_in(key, 505), grid_shape, 0, 4)
    dst_part = jax.random.randint(jax.random.fold_in(key, 606), grid_shape, 0, PDEV)
    dst_side = jax.random.randint(jax.random.fold_in(key, 707), grid_shape, 0, 4)
    src_global = sources[:, None] * PDEV + src_part
    dst_global = targets * PDEV + dst_part
    src_extent = jnp.where(src_side < 2, extents[src_global, 1], extents[src_global, 0])
    dst_extent = jnp.where(dst_side < 2, extents[dst_global, 1], extents[dst_global, 0])
    seg_length = jax.random.randint(jax.random.fold_in(key, 808), grid_shape, 1, jnp.minimum(src_extent, dst_extent) + 1)
    seg_length = jnp.where(alive, seg_length, 0)
    src_start = jax.random.randint(jax.random.fold_in(key, 909), grid_shape, 0, src_extent - seg_length + 1)
    dst_start = jax.random.randint(jax.random.fold_in(key, 1001), grid_shape, 0, dst_extent - seg_length + 1)
    face_rows = jnp.stack([src_part, src_side, src_start, seg_length, targets, dst_part, dst_side, dst_start], -1)
    return (extents.astype(jnp.int32), face_rows.reshape(N_DOM * FDEV, 8).astype(jnp.int32))


def draw_partition_boxes(key, part):
    return layout_tables(key)[0]


def draw_face_table(key, part):
    return layout_tables(key)[1]


def block_levels(stream_key, extent, pieces, smallest, largest):
    def one(dim, parts):
        steps = jax.random.uniform(jax.random.fold_in(jax.random.fold_in(stream_key, 6), dim), (parts,), jnp.float32, smallest / len(pieces), largest / len(pieces))
        return jnp.repeat(jnp.exp(steps), extent[dim] // parts).reshape((-1,) + (1,) * (len(extent) - dim - 1))

    gain = one(*pieces[0])
    for cut in pieces[1:]:
        gain = gain * one(*cut)
    return gain


def centred(own_key, dims, spread, most, pieces=(), held_as=jnp.bfloat16):
    entries = jax.random.normal(own_key, dims, jnp.float32) * spread
    if len(pieces) > 0:
        entries = block_levels(own_key, dims, pieces, -0.22, 0.18) * entries
    return jnp.clip(entries, min=-most, max=most).astype(held_as)


def setup_inputs(seed: int = 0) -> dict:
    arg_keys = jax.random.split(jax.random.key(seed), 5)
    return {
        "modes_now": centred(arg_keys[0], (NZ, PARTS_SIZE, B * B), 1.0, 6.0, ((0, 8), (1, 32)), jnp.float32),
        "modes_prev": centred(arg_keys[1], (NZ, PARTS_SIZE, B * B), 1.0, 6.0, ((0, 8), (1, 32)), jnp.float32),
        "partition_boxes": draw_partition_boxes(jax.random.fold_in(arg_keys[4], 71), 0),
        "face_table": draw_face_table(jax.random.fold_in(arg_keys[4], 71), 0),
    }


COUPLING = 32.0
STENCIL = (COUPLING * 270.0 / 180.0, COUPLING * -27.0 / 180.0, COUPLING * 2.0 / 180.0)
TIME_STEP = 0.4

def cosine_table(lengths, box_side):
    lengths = lengths.astype(jnp.float32)[..., None, None]
    ordinal = jnp.arange(box_side, dtype=jnp.float32)
    waves = ordinal[:, None]
    places = ordinal[None, :]
    scales = jnp.sqrt(jnp.where(waves == 0, 1.0, 2.0) / lengths)
    values = scales * jnp.cos(jnp.pi * waves * (places + 0.5) / lengths)
    inside = (waves < lengths) & (places < lengths)
    return jnp.where(inside, values, 0.0)

def mix_planes(matrix, grid_field):
    flat = grid_field.reshape(matrix.shape[1], -1)
    mixed = jnp.dot(matrix, flat, precision=lax.Precision.HIGHEST, preferred_element_type=jnp.float32)
    return mixed.reshape(matrix.shape[0], grid_field.shape[1], grid_field.shape[2])

def to_cells(table_rows, table_cols, grid_field, box_side):
    planes, holders, cells = grid_field.shape
    squares = grid_field.reshape(planes, holders, box_side, box_side)
    halfway = jnp.einsum('pka,zpkl->zpal', table_rows, squares, precision=lax.Precision.HIGHEST)
    complete = jnp.einsum('zpal,plb->zpab', halfway, table_cols, precision=lax.Precision.HIGHEST)
    return complete.reshape(planes, holders, cells)

def to_modes(table_rows, table_cols, grid_field, box_side):
    planes, holders, cells = grid_field.shape
    squares = grid_field.reshape(planes, holders, box_side, box_side)
    halfway = jnp.einsum('pka,zpab->zpkb', table_rows, squares, precision=lax.Precision.HIGHEST)
    complete = jnp.einsum('zpkb,plb->zpkl', halfway, table_cols, precision=lax.Precision.HIGHEST)
    return complete.reshape(planes, holders, cells)

def side_cells(facing, offsets, amounts, extent_rows, extent_cols, box_side):
    number = facing.shape[0]
    layers = jnp.arange(3, dtype=jnp.int32)[None, :, None]
    position = jnp.arange(box_side, dtype=jnp.int32)[None, None, :]
    facing = facing[:, None, None]
    reached = offsets[:, None, None] + position
    coord_rows = jnp.where(facing == 0, layers, jnp.where(facing == 1, extent_rows[:, None, None] - 1 - layers, reached))
    coord_cols = jnp.where(facing == 2, layers, jnp.where(facing == 3, extent_cols[:, None, None] - 1 - layers, reached))
    usable = jnp.broadcast_to((position < amounts[:, None, None]) & (layers >= 0), (number, 3, box_side))
    cell_index = jnp.where(usable, coord_rows * box_side + coord_cols, 0)
    return (cell_index.reshape(number, 3 * box_side).astype(jnp.int32), usable.reshape(number, 3 * box_side))

def face_forcing(pressure, aligned, targets, facing, offsets, amounts, extent_rows, extent_cols, box_side):
    planes = pressure.shape[0]
    number = targets.shape[0]
    cell_index, usable = side_cells(facing, offsets, amounts, extent_rows[targets], extent_cols[targets], box_side)
    inside_rim = jnp.where(usable, pressure[:, targets[:, None], cell_index], 0.0)
    jumps = (aligned - inside_rim).reshape(planes, number, 3, box_side)
    nearest = jumps[:, :, 0]
    second = jumps[:, :, 1]
    farthest = jumps[:, :, 2]
    closest = STENCIL[0] * nearest + STENCIL[1] * second + STENCIL[2] * farthest
    middle = STENCIL[1] * nearest + STENCIL[2] * second
    outer = STENCIL[2] * nearest
    pushes = jnp.stack([closest, middle, outer], 2).reshape(planes, number, 3 * box_side)
    pushes = jnp.where(usable, pushes, 0.0)
    return jnp.zeros_like(pressure).at[:, targets[:, None], cell_index].add(pushes)

def advance(modes_now, modes_prev, force_modes, extent_rows, extent_cols, first_plane, total_planes, box_side):
    planes, holders, cells = modes_now.shape
    wave_depth = (first_plane + jnp.arange(planes, dtype=jnp.int32)).astype(jnp.float32) / total_planes
    wave_side = jnp.arange(box_side, dtype=jnp.float32)
    float_rows = extent_rows.astype(jnp.float32)
    float_cols = extent_cols.astype(jnp.float32)
    ratio_rows = wave_side[None, :] / float_rows[:, None]
    ratio_cols = wave_side[None, :] / float_cols[:, None]
    squared = jnp.pi ** 2 * (wave_depth[:, None, None, None] ** 2 + ratio_rows[None, :, :, None] ** 2 + ratio_cols[None, :, None, :] ** 2)
    phases = jnp.sqrt(squared) * TIME_STEP
    growth = TIME_STEP * TIME_STEP * jnp.sinc(phases / (2.0 * jnp.pi)) ** 2
    inside = (wave_side[None, :, None] < float_rows[:, None, None]) & (wave_side[None, None, :] < float_cols[:, None, None])
    grid_shape = (planes, holders, box_side, box_side)
    updated = 2.0 * jnp.cos(phases) * modes_now.reshape(grid_shape) - modes_prev.reshape(grid_shape) + growth * force_modes.reshape(grid_shape)
    return jnp.where(inside[None], updated, 0.0).reshape(planes, holders, cells)

def reference(modes_now, modes_prev, partition_boxes, face_table):
    extent_rows = partition_boxes[:, 0]
    extent_cols = partition_boxes[:, 1]
    table_rows = cosine_table(extent_rows, B)
    table_cols = cosine_table(extent_cols, B)
    table_depth = cosine_table(jnp.full((), NZ, jnp.int32), NZ)
    plane_modes = mix_planes(table_depth.T, modes_now)
    pressure = to_cells(table_rows, table_cols, plane_modes, B)
    row_ids = jnp.arange(N_DOM * FDEV, dtype=jnp.int32)
    holder = row_ids // FDEV
    sources = holder * PDEV + face_table[:, 0]
    src_index, src_usable = side_cells(face_table[:, 1], face_table[:, 2], face_table[:, 3], extent_rows[sources], extent_cols[sources], B)
    aligned = jnp.where(src_usable, pressure[:, sources[:, None], src_index], 0.0)
    targets = face_table[:, 4] * PDEV + face_table[:, 5]
    forcing = face_forcing(pressure, aligned, targets, face_table[:, 6], face_table[:, 7], face_table[:, 3], extent_rows, extent_cols, B)
    force_modes = mix_planes(table_depth, to_modes(table_rows, table_cols, forcing, B))
    new_modes = advance(modes_now, modes_prev, force_modes, extent_rows, extent_cols, jnp.zeros((), jnp.int32), NZ, B)
    return (new_modes, pressure)
```

```python
import jax
import jax.numpy as jnp
from jax import lax
from jax.sharding import PartitionSpec as P

B = 64

COUPLING = 32.0
STENCIL = (COUPLING * 270.0 / 180.0, COUPLING * -27.0 / 180.0, COUPLING * 2.0 / 180.0)
TIME_STEP = 0.4
PREC = lax.Precision.HIGH


def cosine_table(lengths, box_side):
    lengths = lengths.astype(jnp.float32)[..., None, None]
    ordinal = jnp.arange(box_side, dtype=jnp.float32)
    waves = ordinal[:, None]
    places = ordinal[None, :]
    scales = jnp.sqrt(jnp.where(waves == 0, 1.0, 2.0) / lengths)
    values = scales * jnp.cos(jnp.pi * waves * (places + 0.5) / lengths)
    inside = (waves < lengths) & (places < lengths)
    return jnp.where(inside, values, 0.0)


def to_cells(table_rows, table_cols, grid_field, box_side):
    planes, holders, cells = grid_field.shape
    squares = grid_field.reshape(planes, holders, box_side, box_side)
    halfway = jnp.einsum("pka,zpkl->zpal", table_rows, squares, precision=PREC)
    complete = jnp.einsum("zpal,plb->zpab", halfway, table_cols, precision=PREC)
    return complete.reshape(planes, holders, cells)


def to_modes(table_rows, table_cols, grid_field, box_side):
    planes, holders, cells = grid_field.shape
    squares = grid_field.reshape(planes, holders, box_side, box_side)
    halfway = jnp.einsum("pka,zpab->zpkb", table_rows, squares, precision=PREC)
    complete = jnp.einsum("zpkb,plb->zpkl", halfway, table_cols, precision=PREC)
    return complete.reshape(planes, holders, cells)


def swap(block, step):
    count = lax.axis_size("height")
    return lax.ppermute(block, "height", [(i, i ^ step) for i in range(count)])


def depth_to_planes(field):
    planes, holders, cells = field.shape
    count = lax.axis_size("height")
    total = planes * count
    mine = lax.axis_index("height")
    part = cells // count
    order = jnp.bitwise_xor(mine, jnp.arange(count, dtype=jnp.int32))
    global_ids = (order[:, None] * planes + jnp.arange(planes, dtype=jnp.int32)).reshape(-1)
    waves = global_ids.astype(jnp.float32)[:, None]
    places = global_ids.astype(jnp.float32)[None, :]
    scales = jnp.sqrt(jnp.where(waves == 0, 1.0, 2.0) / total)
    table = scales * jnp.cos(jnp.pi * waves * (places + 0.5) / total)
    blocks = [
        lax.dynamic_slice_in_dim(field, (mine ^ step) * part, part, 2) for step in range(count)
    ]
    got = [blocks[0]] + [swap(blocks[step], step) for step in range(1, count)]
    gathered = jnp.concatenate(got, 0)
    mixed = jnp.einsum("kz,kpc->zpc", table, gathered, precision=PREC)
    out = [mixed[step * planes : (step + 1) * planes] for step in range(count)]
    back = [out[0]] + [swap(out[step], step) for step in range(1, count)]
    result = jnp.zeros_like(field)
    for step in range(count):
        result = lax.dynamic_update_slice_in_dim(result, back[step], (mine ^ step) * part, 2)
    return result


def side_selectors(extent_rows, extent_cols, box_side):
    holders = extent_rows.shape[0]
    layers = jnp.arange(3, dtype=jnp.int32)[None, :, None]
    place = jnp.arange(box_side, dtype=jnp.int32)[None, None, :]
    lowest = jnp.broadcast_to(place == layers, (holders, 3, box_side))
    high_rows = place == extent_rows[:, None, None] - 1 - layers
    high_cols = place == extent_cols[:, None, None] - 1 - layers
    select_rows = jnp.stack([lowest, high_rows], 1).astype(jnp.float32)
    select_cols = jnp.stack([lowest, high_cols], 1).astype(jnp.float32)
    return (select_rows, select_cols)


def side_stack(pressure, select_rows, select_cols, box_side):
    planes, holders, cells = pressure.shape
    squares = pressure.reshape(planes, holders, box_side, box_side)
    along_cols = jnp.einsum("psjx,zpxy->zpsjy", select_rows, squares, precision=PREC)
    along_rows = jnp.einsum("psjy,zpxy->zpsjx", select_cols, squares, precision=PREC)
    joined = jnp.concatenate([along_cols, along_rows], 2)
    return joined.reshape(planes, holders * 4, 3, box_side)


def pick_rows(row_ids, count):
    return (row_ids[:, None] == jnp.arange(count, dtype=jnp.int32)[None, :]).astype(jnp.float32)


def interfaces(pressure, face_table, extent_rows, extent_cols):
    planes, holders, cells = pressure.shape
    listed = face_table.shape[0]
    dom_count = lax.axis_size("dom")
    pair_most = max(2, listed // dom_count)
    slots = dom_count * pair_most
    select_rows, select_cols = side_selectors(extent_rows, extent_cols, B)
    sides = side_stack(pressure, select_rows, select_cols, B)
    count = sides.shape[1]
    src_start = face_table[:, 2]
    length = face_table[:, 3]
    targets = face_table[:, 4]
    dst_id = face_table[:, 5] * 4 + face_table[:, 6]
    dst_start = face_table[:, 7]
    matches = (targets[:, None] == jnp.arange(dom_count, dtype=jnp.int32)[None, :]).astype(
        jnp.int32
    )
    position_in = jnp.sum(jnp.cumsum(matches, 0) * matches, 1) - 1
    slot_ids = targets * pair_most + position_in
    slot_hits = (
        jnp.arange(slots, dtype=jnp.int32)[:, None] == slot_ids[None, :]
    ).astype(jnp.float32)
    place = jnp.arange(B, dtype=jnp.int32)
    covered = (place[None, :] >= dst_start[:, None]) & (
        place[None, :] < (dst_start + length)[:, None]
    )
    shift = (place[None, None, :] == place[None, :, None] + (src_start - dst_start)[:, None, None])
    shift = (shift & covered[:, :, None]).astype(jnp.float32)
    source_hits = slot_hits @ pick_rows(face_table[:, 0] * 4 + face_table[:, 1], count)
    picked = jnp.einsum("sk,zkjc->zsjc", source_hits, sides, precision=PREC)
    slot_shift = jnp.einsum("sr,rqc->sqc", slot_hits, shift)
    outgoing = jnp.einsum("sqc,zsjc->zsjq", slot_shift, picked, precision=PREC)
    codes = jnp.where(covered, (dst_id + 1)[:, None], 0).astype(jnp.float32)
    slot_codes = jnp.einsum("sr,rq->sq", slot_hits, codes)
    slot_codes = jnp.broadcast_to(slot_codes[None, :, None, :], (planes, slots, 1, B))
    payload = jnp.concatenate([outgoing, slot_codes], 2).reshape(planes, slots, 4 * B)
    arrived = lax.all_to_all(payload, "dom", split_axis=1, concat_axis=1, tiled=True)
    arrived = arrived.reshape(planes, slots, 4, B)
    mask_codes = arrived[0, :, 3].astype(jnp.int32)
    hits = (mask_codes[:, None, :] == jnp.arange(1, count + 1, dtype=jnp.int32)[None, :, None])
    hits = hits.astype(jnp.float32)
    times = jnp.sum(hits, 0)
    slot_id = jnp.max(mask_codes, 1)
    owner = pick_rows(slot_id - 1, count)
    incoming = jnp.einsum("sk,zsjc->zkjc", owner, arrived[:, :, :3], precision=PREC)
    jumps = incoming - times[None, :, None, :] * sides
    nearest = jumps[:, :, 0]
    second = jumps[:, :, 1]
    farthest = jumps[:, :, 2]
    closest = STENCIL[0] * nearest + STENCIL[1] * second + STENCIL[2] * farthest
    middle = STENCIL[1] * nearest + STENCIL[2] * second
    outer = STENCIL[2] * nearest
    side_force = jnp.stack([closest, middle, outer], 2)
    return side_force.reshape(planes, holders, 4, 3, B), select_rows, select_cols


def spread_modes(side_force, select_rows, select_cols, table_rows, table_cols):
    planes, holders = side_force.shape[:2]
    wave_y = jnp.einsum("zpsjy,ply->zpsjl", side_force[:, :, 0:2], table_cols, precision=PREC)
    wave_x = jnp.einsum("zpsjx,pkx->zpsjk", side_force[:, :, 2:4], table_rows, precision=PREC)
    edge_x = jnp.einsum("psjx,pkx->psjk", select_rows, table_rows, precision=lax.Precision.HIGHEST)
    edge_y = jnp.einsum("psjy,ply->psjl", select_cols, table_cols, precision=lax.Precision.HIGHEST)
    wide = (planes, holders, 6, B)
    left = jnp.concatenate(
        [jnp.broadcast_to(edge_x.reshape(1, holders, 6, B), wide), wave_x.reshape(wide)], 2
    )
    right = jnp.concatenate(
        [wave_y.reshape(wide), jnp.broadcast_to(edge_y.reshape(1, holders, 6, B), wide)], 2
    )
    both = jnp.einsum("zpjk,zpjl->zpkl", left, right, precision=PREC)
    return both.reshape(planes, holders, B * B)


def advance(
    modes_now,
    modes_prev,
    force_modes,
    extent_rows,
    extent_cols,
    first_plane,
    total_planes,
    box_side,
):
    planes, holders, cells = modes_now.shape
    wave_depth = (first_plane + jnp.arange(planes, dtype=jnp.int32)).astype(
        jnp.float32
    ) / total_planes
    wave_side = jnp.arange(box_side, dtype=jnp.float32)
    float_rows = extent_rows.astype(jnp.float32)
    float_cols = extent_cols.astype(jnp.float32)
    ratio_rows = wave_side[None, :] / float_rows[:, None]
    ratio_cols = wave_side[None, :] / float_cols[:, None]
    squared = jnp.pi**2 * (
        wave_depth[:, None, None, None] ** 2
        + ratio_rows[None, :, :, None] ** 2
        + ratio_cols[None, :, None, :] ** 2
    )
    phases = jnp.sqrt(squared) * TIME_STEP
    growth = TIME_STEP * TIME_STEP * jnp.sinc(phases / (2.0 * jnp.pi)) ** 2
    inside = (wave_side[None, :, None] < float_rows[:, None, None]) & (
        wave_side[None, None, :] < float_cols[:, None, None]
    )
    grid_shape = (planes, holders, box_side, box_side)
    updated = (
        2.0 * jnp.cos(phases) * modes_now.reshape(grid_shape)
        - modes_prev.reshape(grid_shape)
        + growth * force_modes.reshape(grid_shape)
    )
    return jnp.where(inside[None], updated, 0.0).reshape(planes, holders, cells)


def on_device(modes_now, modes_prev, partition_boxes, face_table):
    planes = modes_now.shape[0]
    total_planes = planes * lax.axis_size("height")
    extent_rows = partition_boxes[:, 0]
    extent_cols = partition_boxes[:, 1]
    table_rows = cosine_table(extent_rows, B)
    table_cols = cosine_table(extent_cols, B)
    in_cells = to_cells(table_rows, table_cols, modes_now, B)
    pressure = depth_to_planes(in_cells)
    side_force, select_rows, select_cols = interfaces(
        in_cells, face_table, extent_rows, extent_cols
    )
    force_modes = spread_modes(side_force, select_rows, select_cols, table_rows, table_cols)
    first_plane = lax.axis_index("height") * planes
    new_modes = advance(
        modes_now, modes_prev, force_modes, extent_rows, extent_cols, first_plane, total_planes, B
    )
    return (new_modes, pressure)


def solution(mesh):
    placed = (P("height", "dom", None), P("height", "dom", None), P("dom", None), P("dom", None))
    return jax.shard_map(
        on_device,
        mesh=mesh,
        in_specs=placed,
        out_specs=(P("height", "dom", None), P("height", "dom", None)),
        check_vma=False,
    )
```

```python
import functools

import jax
import jax.numpy as jnp
import numpy as np
from jax import lax
from jax.experimental import pallas as pl
from jax.experimental.pallas import tpu as pltpu
from jax.sharding import PartitionSpec as P


B = 64
LANES = 128
UNROLL_A = 1
UNROLL_B = 1
RIM = 8

COUPLING = 32.0
STENCIL = (COUPLING * 270.0 / 180.0, COUPLING * -27.0 / 180.0, COUPLING * 2.0 / 180.0)
TIME_STEP = 0.4


bf16 = jnp.bfloat16
f32 = jnp.float32


def cosine(length, wave, place):
    angle = wave * (2 * place + 1)
    period = 4 * length
    turns = jnp.floor((angle.astype(f32) + 0.5) / period.astype(f32)).astype(jnp.int32)
    angle = angle - turns * period
    angle = jnp.minimum(angle, period - angle)
    x = (length - angle).astype(f32) * ((np.pi / 2) / length.astype(f32))
    y = x * x
    s = f32(-2.50521084e-8)
    for c in (2.75573192e-6, -1.98412698e-4, 8.33333333e-3, -1.66666667e-1):
        s = s * y + f32(c)
    s = x + x * y * s
    scale = jnp.sqrt(jnp.where(wave == 0, 1.0, 2.0) / length.astype(f32))
    inside = (wave < length) & (place < length) & (place >= 0)
    return jnp.where(inside, scale * s, 0.0)


def iota(shape, axis):
    return lax.broadcasted_iota(jnp.int32, shape, axis)


def rim_cell(index, extent):
    return jnp.where(index < 3, index, jnp.where(index < 6, extent + 2 - index, -1))


def split(x):
    hi = x.astype(bf16)
    lo = (x - hi.astype(f32)).astype(bf16)
    return hi, lo


def dot(a, b):
    return jnp.dot(a, b, preferred_element_type=f32)


def backward_tables(extent_rows, extent_cols):
    count = extent_rows.shape[0]
    ex = extent_rows[:, None, None]
    ey = extent_cols[:, None, None]
    shape = (count, B, LANES)
    col_back = cosine(ey, iota(shape, 2) % B, iota(shape, 1))
    row = iota(shape, 1)
    lane = iota(shape, 2)
    row_back = jnp.where(lane < B, cosine(ex, 2 * (row % 32) + row // 32, lane), 0.0)

    def edge(extent, wave, index):
        layer = index % 3
        total = jnp.zeros(wave.shape, f32)
        for i in range(3):
            cell = jnp.where(index < 3, i, extent - 1 - i)
            weight = jnp.where(
                i + layer == 0,
                STENCIL[0],
                jnp.where(i + layer == 1, STENCIL[1], jnp.where(i + layer == 2, STENCIL[2], 0.0)),
            )
            total = total + weight * cosine(extent, wave, cell)
        return jnp.where(index < 6, total, 0.0)

    shape = (count, 32, LANES)
    lane = iota(shape, 2)
    edge_rows = edge(ex, 2 * iota(shape, 1) + (lane // 8) % 2, lane % 8)
    shape = (count, 16, LANES)
    row = iota(shape, 1)
    lane = iota(shape, 2)
    edge_cols = jnp.where(row // 8 == lane // B, edge(ey, lane % B, row % 8), 0.0)
    return col_back, row_back, edge_rows, edge_cols


def cosine_tile(length, wave, place):
    size = jnp.full((1, LANES), length, jnp.int32).astype(f32)
    unit = 1.0 / size
    angle = wave * (2.0 * place + 1.0)
    angle = angle - jnp.floor((angle + 0.5) * (0.25 * unit)) * (4.0 * size)
    angle = jnp.minimum(angle, 4.0 * size - angle)
    x = (size - angle) * (f32(np.pi / 2) * unit)
    y = x * x
    s = f32(-2.50521084e-8)
    for c in (2.75573192e-6, -1.98412698e-4, 8.33333333e-3, -1.66666667e-1):
        s = s * y + f32(c)
    s = x + x * y * s
    s = s * jnp.where(wave == 0.0, jnp.sqrt(unit), jnp.sqrt(2.0 * unit))
    return jnp.where((wave < size) & (place < size) & (place >= 0.0), s, 0.0)


def cells_kernel(
    planes, mine_ref, box_ref, face_ref, x_ref, piece_ref, rim_ref, pay_ref, used_ref, table_ref
):
    mine = mine_ref[0]
    holders = box_ref.shape[0]
    lane = iota((B, LANES), 1)
    low = lane < B
    low32 = iota((32, LANES), 1) < B
    low8 = iota((8, LANES), 1) < B
    row64 = iota((B, LANES), 0).astype(f32)
    x_wave = 2 * (lane % 32) + (lane // 32) % 2
    x_wave64 = x_wave.astype(f32)
    x_wave8 = x_wave[:8].astype(f32)

    def one(p, carry):
        x = jnp.concatenate(
            [x_ref[pl.ds(kz * 256 + p, 32, stride=8), :] for kz in range(planes)], 0
        )
        ex = box_ref[p, 0]
        ey = box_ref[p, 1]
        c = cosine_tile(
            ey, row64, jnp.where(low, lane, rim_cell(lane - B, ey)).astype(f32)
        )
        spot = pl.multiple_of(p * B, B)
        g = cosine_tile(ex, x_wave64, row64)
        table_ref[pl.ds(spot, B), :] = g
        edge = cosine_tile(ex, x_wave8, rim_cell(iota((8, LANES), 0), ex).astype(f32))
        rows = jnp.concatenate(
            [
                table_ref[pl.ds(spot, 32, stride=2), :],
                pltpu.roll(table_ref[pl.ds(spot + 1, 32, stride=2), :], 32, 1),
                edge,
                jnp.zeros((8, LANES), f32),
                g,
                jnp.zeros((B, LANES), f32),
            ],
            0,
        )
        turned = pltpu.roll(c, B, 1)
        c = jnp.concatenate(
            [
                jnp.concatenate([jnp.where(low, c, 0.0), jnp.where(low, turned, 0.0)], 1),
                jnp.concatenate([jnp.where(low, 0.0, turned), jnp.where(low, 0.0, c)], 1),
            ],
            0,
        )
        c_hi, c_lo = split(c)
        x_hi, x_lo = split(x)
        t = dot(
            jnp.concatenate([x_hi, x_hi, x_lo], 1), jnp.concatenate([c_hi, c_lo, c_hi], 0)
        )
        main = [t[kz * 32 : (kz + 1) * 32, :LANES] for kz in range(planes)]
        rims = t[0:32, LANES:]
        for kz in range(1, planes):
            rims = rims + pltpu.roll(t[kz * 32 : (kz + 1) * 32, LANES:], kz * RIM, 1)
        main.append(rims)
        upper = jnp.concatenate(main, 1)
        lower = jnp.concatenate([pltpu.roll(m, B, 1) for m in main], 1)
        r_hi, r_lo = split(jnp.concatenate([upper, lower], 0))
        right = jnp.concatenate([r_hi, r_lo, r_hi, r_lo], 0)
        l_hi, l_lo = split(rows)
        l_lo = jnp.where(iota((208, LANES), 1) < B, l_lo, jnp.zeros_like(l_lo))
        left = jnp.concatenate([l_hi, l_lo], 1)
        y = dot(left[:80], right[:, : planes * LANES])
        z = dot(left[80:], right[:, planes * LANES :])
        for kz in range(planes):
            tile = y[:, kz * LANES : (kz + 1) * LANES]
            out = jnp.where(low32, tile[:32], tile[32:64])
            for g in range(8):
                spot = (mine ^ g) * 256 + kz * 32 + p
                piece_ref[pl.ds(spot, 4, stride=8), :] = out[g * 4 : (g + 1) * 4]
            rim_ref[pl.ds(pl.multiple_of(p * 128 + kz * RIM, RIM), RIM), :] = jnp.where(
                low8, tile[64:72], 0.0
            )
        rim_ref[pl.ds(pl.multiple_of(p * 128 + 64, 64), 64), :] = z.T[:64]
        return carry

    lax.fori_loop(0, holders, one, 0, unroll=UNROLL_A)

    pay_ref[...] = jnp.zeros_like(pay_ref)
    targets = pay_ref.shape[0] // 32

    def clear(t, carry):
        used_ref[t] = 0
        return carry

    lax.fori_loop(0, targets, clear, 0)

    def face(r, carry):
        length = face_ref[r, 3]

        @pl.when(length > 0)
        def _():
            side = face_ref[r, 1]
            start = face_ref[r, 2]
            target = face_ref[r, 4]
            code = face_ref[r, 5] * 4 + face_ref[r, 6] + 1
            slot = used_ref[target]
            used_ref[target] = slot + 1
            first = slot * B + face_ref[r, 7]
            turn = (first - start + LANES) & (LANES - 1)
            base = face_ref[r, 0] * 128 + (side >> 1) * 64 + (side & 1) * 3
            lane = iota((RIM, LANES), 1)
            here = (lane >= first) & (lane < first + length)
            for j in range(3):
                values = rim_ref[pl.ds(base + j, planes, stride=RIM), :]
                values = jnp.where(here, pltpu.roll(values, turn, 1), 0.0)
                rows = pl.ds(pl.multiple_of(target * 32 + j * 8, 8), 8)
                pay_ref[rows, :] = pay_ref[rows, :] + values
            rows = pl.ds(pl.multiple_of(target * 32 + 24, 8), 8)
            pay_ref[rows, :] = pay_ref[rows, :] + jnp.where(here, code, 0).astype(f32)

        return carry

    lax.fori_loop(0, face_ref.shape[0], face, 0)


def depth_kernel(planes, table_ref, *refs):
    blocks, out_ref = refs[:-1], refs[-1]
    count = len(blocks)
    total = count * planes
    t_hi, t_lo = split(table_ref[...])
    t_lo = jnp.where(iota((total, LANES), 1) < total, t_lo, jnp.zeros_like(t_lo))
    left = jnp.concatenate([t_hi, t_lo], 1)
    for q in range(4):
        right = jnp.concatenate(
            [
                jnp.concatenate(
                    [b[pl.ds(q * 8 + p, planes, stride=32), :] for b in blocks], 0
                )
                for p in range(8)
            ],
            1,
        )
        r_hi, r_lo = split(right)
        mixed = dot(left, jnp.concatenate([r_hi, r_lo, r_hi, r_lo], 0))
        for p in range(8):
            for s in range(count):
                out_ref[pl.ds(s * 256 + q * 8 + p, planes, stride=32), :] = mixed[
                    s * planes : (s + 1) * planes, p * LANES : (p + 1) * LANES
                ]


def advance_kernel(
    planes,
    total,
    code_ref,
    mine_ref,
    box_ref,
    got_ref,
    rim_ref,
    now_ref,
    prev_ref,
    col_ref,
    row_ref,
    edge_row_ref,
    edge_col_ref,
    out_ref,
    sum_ref,
    times_ref,
):
    holders = col_ref.shape[0]
    sum_ref[...] = jnp.zeros_like(sum_ref)
    times_ref[...] = jnp.zeros_like(times_ref)

    def gather(k, carry):
        code = code_ref[k]

        @pl.when(code > 0)
        def _():
            source = k >> 1
            turn = (k & 1) * B
            which = code - 1
            tile = which >> 1
            first = (which & 1) * 3
            marks = pltpu.roll(got_ref[pl.ds(pl.multiple_of(source * 32 + 24, 8), 8), :], turn, 1)
            here = (marks == code.astype(f32)) & (iota((RIM, LANES), 1) < B)
            for j in range(3):
                values = got_ref[pl.ds(pl.multiple_of(source * 32 + j * 8, 8), 8), :]
                values = jnp.where(here, pltpu.roll(values, turn, 1), 0.0)
                rows = pl.ds(tile * 64 + first + j, planes, stride=RIM)
                sum_ref[rows, :] = sum_ref[rows, :] + values
            row = iota((RIM, LANES), 0)
            hit = here & (row >= first) & (row < first + 3)
            rows = pl.ds(pl.multiple_of(tile * RIM, RIM), RIM)
            times_ref[rows, :] = times_ref[rows, :] + jnp.where(hit, 1.0, 0.0)

        return carry

    lax.fori_loop(0, code_ref.shape[0], gather, 0)
    first_plane = mine_ref[0] * planes

    def one(p, carry):
        jumps = []
        for axis in range(2):
            rows = pl.ds(pl.multiple_of((p * 2 + axis) * 64, 64), 64)
            times = times_ref[pl.ds(pl.multiple_of((p * 2 + axis) * RIM, RIM), RIM), :]
            times = jnp.concatenate([times] * planes, 0)
            jumps.append(split(sum_ref[rows, :] - times * rim_ref[rows, :]))
        j_hi, j_lo = jumps[0]
        c_hi, c_lo = split(jnp.concatenate([col_ref[p], jnp.zeros((B, LANES), f32)], 0))
        along_y = dot(
            jnp.concatenate([j_hi, j_hi, j_lo], 1), jnp.concatenate([c_hi, c_lo, c_hi], 0)
        )
        j_hi, j_lo = jumps[1]
        r_hi, r_lo = split(row_ref[p])
        along_x = lax.dot_general(
            jnp.concatenate([r_hi, r_lo, r_hi], 1),
            jnp.concatenate([j_hi, j_hi, j_lo], 1),
            (((1,), (1,)), ((), ())),
            preferred_element_type=f32,
        )
        along_x = jnp.concatenate([along_x, along_x], 1)
        even, odd = along_x[:32], along_x[32:]
        lane = iota((32, LANES), 1)
        edge = edge_row_ref[p]
        left = []
        for kz in range(planes):
            across = jnp.where(lane // 16 == kz, edge, 0.0)
            back = (LANES - kz * RIM) % LANES
            low = pltpu.roll(even, back, 1) if back else even
            high = pltpu.roll(odd, (back + RIM) % LANES, 1)
            down = jnp.where(lane < RIM, low, jnp.where(lane < 2 * RIM, high, 0.0))
            left.append(jnp.concatenate([across, down], 1))
        left = jnp.concatenate(left, 0)
        half = iota((RIM, LANES), 1) < B
        right = []
        for kz in range(planes):
            tile = along_y[kz * RIM : (kz + 1) * RIM]
            right += [jnp.where(half, tile, 0.0), jnp.where(half, 0.0, tile)]
        right += [edge_col_ref[p], jnp.zeros((LANES - 2 * RIM, LANES), f32)]
        right = jnp.concatenate(right, 0)
        l_hi, l_lo = split(left)
        r_hi, r_lo = split(right)
        force = dot(l_hi, r_hi) + dot(l_hi, r_lo) + dot(l_lo, r_hi)
        ex = box_ref[p, 0]
        ey = box_ref[p, 1]
        wave_x = 2 * iota((32, LANES), 0) + lane // B
        wave_y = lane % B
        inside = (wave_x < ex) & (wave_y < ey)
        unit = TIME_STEP * np.pi
        scale_x = unit / jnp.full((32, LANES), ex, jnp.int32).astype(f32)
        scale_y = unit / jnp.full((32, LANES), ey, jnp.int32).astype(f32)
        flat = (wave_x.astype(f32) * scale_x) ** 2 + (wave_y.astype(f32) * scale_y) ** 2
        for kz in range(planes):
            depth = (first_plane + kz).astype(f32) * (unit / total)
            u = flat + depth * depth
            s = f32(-2.0 / 6402373705728000.0)
            for c in (
                2.0 / 20922789888000.0,
                -2.0 / 87178291200.0,
                2.0 / 479001600.0,
                -2.0 / 3628800.0,
                2.0 / 40320.0,
                -2.0 / 720.0,
                2.0 / 24.0,
            ):
                s = s * u + f32(c)
            s = 1.0 - u * s
            rows = pl.ds(kz * 256 + p, 32, stride=8)
            new = (2.0 - u * s) * now_ref[rows, :] - prev_ref[rows, :]
            new = new + (TIME_STEP * TIME_STEP) * s * force[kz * 32 : (kz + 1) * 32]
            out_ref[rows, :] = jnp.where(inside, new, 0.0)
        return carry

    lax.fori_loop(0, holders, one, 0, unroll=UNROLL_B)


def join_kernel(planes, mine_ref, *refs):
    blocks, out_ref = refs[:-1], refs[-1]
    mine = mine_ref[0]
    for s, block in enumerate(blocks):
        for z in range(planes):
            spot = pl.multiple_of((mine ^ s) * 32 + z * 256, 32)
            out_ref[pl.ds(spot, 32), :] = block[z * 32 : (z + 1) * 32, :]


VM = pl.BlockSpec(memory_space=pltpu.VMEM)
SM = pl.BlockSpec(memory_space=pltpu.SMEM)


def call(kernel, args, spots, outs, scratch=(), flops=10**8):
    return pl.pallas_call(
        kernel,
        out_shape=outs,
        in_specs=spots,
        out_specs=jax.tree.map(lambda _: VM, outs),
        scratch_shapes=list(scratch),
        compiler_params=pltpu.CompilerParams(vmem_limit_bytes=40 * 2**20),
        cost_estimate=pl.CostEstimate(flops=flops, bytes_accessed=4 * 2**20, transcendentals=0),
    )(*args)


def swap(block, step):
    count = lax.axis_size("height")
    return lax.ppermute(block, "height", [(i, i ^ step) for i in range(count)])


def tiles(field):
    planes, holders, cells = field.shape
    split_up = field.reshape(planes, holders, cells // LANES, LANES).transpose(0, 2, 1, 3)
    return split_up.reshape(-1, LANES)


def untiles(rows, planes, holders):
    cells = rows.shape[0] // (planes * holders)
    folded = rows.reshape(planes, cells, holders, LANES).transpose(0, 2, 1, 3)
    return folded.reshape(planes, holders, cells * LANES)


def step(modes_now, modes_prev, partition_boxes, face_table):
    planes, holders, _ = modes_now.shape
    count = lax.axis_size("height")
    domains = lax.axis_size("dom")
    total = planes * count
    mine = lax.axis_index("height").astype(jnp.int32)
    extent_rows = partition_boxes[:, 0]
    extent_cols = partition_boxes[:, 1]
    now = tiles(modes_now)
    prev = tiles(modes_prev)
    mine_word = mine.reshape(1)

    def rows(n):
        return jax.ShapeDtypeStruct((n, LANES), f32)

    pieces, rim, pay = call(
        functools.partial(cells_kernel, planes),
        (mine_word, partition_boxes, face_table, now),
        [SM, SM, SM, VM],
        (rows(2048), rows(holders * 128), rows(domains * 32)),
        [pltpu.SMEM((domains,), jnp.int32), pltpu.VMEM((holders * B, LANES), f32)],
    )
    pieces = pieces.reshape(count, 256, LANES)
    got = [pieces[0]] + [swap(pieces[s], s) for s in range(1, count)]
    arrived = lax.all_to_all(pay.reshape(domains, 32, LANES), "dom", 0, 0, tiled=True)

    order = (mine ^ jnp.arange(count, dtype=jnp.int32))[:, None] * planes
    order = (order + jnp.arange(planes, dtype=jnp.int32)).reshape(-1)
    depth_table = cosine(jnp.full((), total, jnp.int32), order[None, :], order[:, None])
    depth_table = jnp.concatenate([depth_table, depth_table], 1)
    mixed = call(
        functools.partial(depth_kernel, planes), (depth_table, *got), [VM] * (1 + count), rows(2048)
    )
    mixed = mixed.reshape(count, 256, LANES)
    back = [mixed[0]] + [swap(mixed[s], s) for s in range(1, count)]

    codes = jnp.max(arrived[:, 24].reshape(domains * 2, B), 1).astype(jnp.int32)
    new = call(
        functools.partial(advance_kernel, planes, total),
        (codes, mine_word, partition_boxes, arrived.reshape(-1, LANES), rim, now, prev)
        + tuple(backward_tables(extent_rows, extent_cols)),
        [SM] * 3 + [VM] * 8,
        rows(2048),
        [pltpu.VMEM((holders * 128, LANES), f32), pltpu.VMEM((holders * 2 * RIM, LANES), f32)],
    )
    pressure = call(
        functools.partial(join_kernel, planes), (mine_word, *back), [SM] + [VM] * count, rows(2048)
    )
    pressure = untiles(pressure, planes, holders)
    return untiles(new, planes, holders), pressure


def solution(mesh):
    placed = (P("height", "dom", None), P("height", "dom", None), P("dom", None), P("dom", None))
    return jax.shard_map(
        step,
        mesh=mesh,
        in_specs=placed,
        out_specs=(P("height", "dom", None), P("height", "dom", None)),
        check_vma=False,
    )
```

```python
import functools

import jax
import jax.numpy as jnp
import numpy as np
from jax import lax
from jax.experimental import pallas as pl
from jax.experimental.pallas import tpu as pltpu
from jax.sharding import PartitionSpec as P


B = 64
LANES = 128
FACE_ROWS = 25
RIM = 8

COUPLING = 32.0
STENCIL = (COUPLING * 270.0 / 180.0, COUPLING * -27.0 / 180.0, COUPLING * 2.0 / 180.0)
TIME_STEP = 0.4
WAVE = (
    0.9999999998806415,
    -0.08333333151883045,
    0.002777773302928117,
    -4.959913250130888e-05,
    5.494915434656933e-07,
    -3.861085658928547e-09,
)


bf16 = jnp.bfloat16
f32 = jnp.float32


def cosine(length, wave, place):
    angle = wave * (2 * place + 1)
    period = 4 * length
    turns = jnp.floor((angle.astype(f32) + 0.5) / period.astype(f32)).astype(jnp.int32)
    angle = angle - turns * period
    angle = jnp.minimum(angle, period - angle)
    x = (length - angle).astype(f32) * ((np.pi / 2) / length.astype(f32))
    y = x * x
    s = f32(-2.50521084e-8)
    for c in (2.75573192e-6, -1.98412698e-4, 8.33333333e-3, -1.66666667e-1):
        s = s * y + f32(c)
    s = x + x * y * s
    scale = jnp.sqrt(jnp.where(wave == 0, 1.0, 2.0) / length.astype(f32))
    inside = (wave < length) & (place < length) & (place >= 0)
    return jnp.where(inside, scale * s, 0.0)


def iota(shape, axis):
    return lax.broadcasted_iota(jnp.int32, shape, axis)


def rim_cell(index, extent):
    return jnp.where(index < 3, index, jnp.where(index < 6, extent + 2 - index, -1))


def split(x):
    hi = x.astype(bf16)
    lo = (x - hi.astype(f32)).astype(bf16)
    return hi, lo


def dot(a, b):
    return jnp.dot(a, b, preferred_element_type=f32)


def backward_tables(extent_rows, extent_cols):
    count = extent_rows.shape[0]
    ex = extent_rows[:, None, None]
    ey = extent_cols[:, None, None]
    shape = (count, B, LANES)
    col_back = cosine(ey, iota(shape, 2) % B, iota(shape, 1))
    row = iota(shape, 1)
    lane = iota(shape, 2)
    row_back = jnp.where(lane < B, cosine(ex, 2 * (row % 32) + row // 32, lane), 0.0)

    def edge(extent, wave, index):
        layer = index % 3
        total = jnp.zeros(wave.shape, f32)
        for i in range(3):
            cell = jnp.where(index < 3, i, extent - 1 - i)
            weight = jnp.where(
                i + layer == 0,
                STENCIL[0],
                jnp.where(i + layer == 1, STENCIL[1], jnp.where(i + layer == 2, STENCIL[2], 0.0)),
            )
            total = total + weight * cosine(extent, wave, cell)
        return jnp.where(index < 6, total, 0.0)

    shape = (count, 32, LANES)
    lane = iota(shape, 2)
    edge_rows = edge(ex, 2 * iota(shape, 1) + (lane // 8) % 2, lane % 8)
    shape = (count, 16, LANES)
    row = iota(shape, 1)
    lane = iota(shape, 2)
    edge_cols = jnp.where(row // 8 == lane // B, edge(ey, lane % B, row % 8), 0.0)
    return col_back, row_back, edge_rows, edge_cols


def cosine_tile(length, wave, place):
    size = jnp.full((1, LANES), length, jnp.int32).astype(f32)
    unit = 1.0 / size
    angle = wave * (2.0 * place + 1.0)
    angle = angle - jnp.floor((angle + 0.5) * (0.25 * unit)) * (4.0 * size)
    angle = jnp.minimum(angle, 4.0 * size - angle)
    x = (size - angle) * (f32(np.pi / 2) * unit)
    y = x * x
    s = f32(-2.50521084e-8)
    for c in (2.75573192e-6, -1.98412698e-4, 8.33333333e-3, -1.66666667e-1):
        s = s * y + f32(c)
    s = x + x * y * s
    s = s * jnp.where(wave == 0.0, jnp.sqrt(unit), jnp.sqrt(2.0 * unit))
    return jnp.where((wave < size) & (place < size) & (place >= 0.0), s, 0.0)


def cells_kernel(
    planes,
    mine_ref,
    box_ref,
    x_hbm,
    piece_ref,
    rim_ref,
    x_ref,
    table_ref,
    c_hi_ref,
    c_lo_ref,
    l_hi_ref,
    l_lo_ref,
    even_hi_ref,
    even_lo_ref,
    odd_hi_ref,
    odd_lo_ref,
    sem,
):
    mine = mine_ref[0]
    holders = box_ref.shape[0]
    fetch = pltpu.make_async_copy(x_hbm, x_ref, sem)
    fetch.start()
    low32 = iota((32, LANES), 1) < B
    low8 = iota((8, LANES), 1) < B
    lane = iota((B, LANES), 1)
    low = lane < B
    row64 = iota((B, LANES), 0).astype(f32)
    x_wave = 2 * (lane % 32) + (lane // 32) % 2
    x_wave64 = x_wave.astype(f32)
    x_wave8 = x_wave[:8].astype(f32)
    l_low = iota((144, LANES), 1) < B

    def tables(p, carry):
        ex = box_ref[p, 0]
        ey = box_ref[p, 1]
        c = cosine_tile(ey, row64, jnp.where(low, lane, rim_cell(lane - B, ey)).astype(f32))
        turned = pltpu.roll(c, B, 1)
        c = jnp.concatenate(
            [
                jnp.concatenate([jnp.where(low, c, 0.0), jnp.where(low, turned, 0.0)], 1),
                jnp.concatenate([jnp.where(low, 0.0, turned), jnp.where(low, 0.0, c)], 1),
            ],
            0,
        )
        c_hi_ref[p], c_lo_ref[p] = split(c)
        spot = pl.multiple_of(p * B, B)
        g = cosine_tile(ex, x_wave64, row64)
        table_ref[pl.ds(spot, B), :] = g
        edge = cosine_tile(ex, x_wave8, rim_cell(iota((8, LANES), 0), ex).astype(f32))
        rows = jnp.concatenate(
            [
                table_ref[pl.ds(spot, 32, stride=2), :],
                pltpu.roll(table_ref[pl.ds(spot + 1, 32, stride=2), :], 32, 1),
                edge,
                jnp.zeros((8, LANES), f32),
                g,
            ],
            0,
        )
        l_hi, l_lo = split(rows)
        l_hi_ref[p] = l_hi
        l_lo_ref[p] = jnp.where(l_low, l_lo, jnp.zeros_like(l_lo))
        return carry

    lax.fori_loop(0, holders, tables, 0)
    fetch.wait()

    def along_y(p, r_hi_ref, r_lo_ref):
        x = jnp.concatenate(
            [x_ref[pl.ds(kz * 256 + p, 32, stride=8), :] for kz in range(planes)], 0
        )
        c_hi, c_lo = c_hi_ref[p], c_lo_ref[p]
        x_hi, x_lo = split(x)
        t = dot(
            jnp.concatenate([x_hi, x_hi, x_lo], 1), jnp.concatenate([c_hi, c_lo, c_hi], 0)
        )
        main = [t[kz * 32 : (kz + 1) * 32, :LANES] for kz in range(planes)]
        rims = t[0:32, LANES:]
        for kz in range(1, planes):
            rims = rims + pltpu.roll(t[kz * 32 : (kz + 1) * 32, LANES:], kz * RIM, 1)
        main.append(rims)
        for i, part in enumerate(main):
            hi, lo = split(jnp.concatenate([part, pltpu.roll(part, B, 1)], 0))
            r_hi_ref[:, i * LANES : (i + 1) * LANES] = hi
            r_lo_ref[:, i * LANES : (i + 1) * LANES] = lo

    def along_x(p, r_hi_ref, r_lo_ref):
        r_hi, r_lo = r_hi_ref[...], r_lo_ref[...]
        right = jnp.concatenate([r_hi, r_lo, r_hi, r_lo], 0)
        left = jnp.concatenate([l_hi_ref[p], l_lo_ref[p]], 1)
        y = dot(left[:80], right[:, : planes * LANES])
        z = dot(left[80:], right[:, planes * LANES :])
        for kz in range(planes):
            tile = y[:, kz * LANES : (kz + 1) * LANES]
            out = jnp.where(low32, tile[:32], tile[32:64])
            for g in range(8):
                spot = (mine ^ g) * 256 + kz * 32 + p
                piece_ref[pl.ds(spot, 4, stride=8), :] = out[g * 4 : (g + 1) * 4]
            rim_ref[pl.ds(pl.multiple_of(p * 128 + kz * RIM, RIM), RIM), :] = jnp.where(
                low8, tile[64:72], 0.0
            )
        rim_ref[pl.ds(pl.multiple_of(p * 128 + 64, 64), 64), :] = jnp.concatenate(
            [z.T[:64], jnp.zeros((64, 64), f32)], 1
        )

    even = (even_hi_ref, even_lo_ref)
    odd = (odd_hi_ref, odd_lo_ref)

    def two(i, carry):
        along_y(2 * i, *even)
        along_x(jnp.maximum(2 * i - 1, 0), *odd)
        along_y(2 * i + 1, *odd)
        along_x(2 * i, *even)
        return carry

    lax.fori_loop(0, holders // 2, two, 0)
    along_x(holders - 1, *odd)


def pack_kernel(planes, face_ref, rim_ref, pay_hbm, used_ref, pay_ref, sem):
    pay_ref[...] = jnp.zeros_like(pay_ref)
    targets = pay_ref.shape[0] // FACE_ROWS

    def clear(t, carry):
        used_ref[t] = 0
        return carry

    lax.fori_loop(0, targets, clear, 0)

    def face(r, carry):
        length = face_ref[r, 3]

        @pl.when(length > 0)
        def _():
            side = face_ref[r, 1]
            start = face_ref[r, 2]
            target = face_ref[r, 4]
            code = face_ref[r, 5] * 4 + face_ref[r, 6] + 1
            slot = used_ref[target]
            used_ref[target] = slot + 1
            first = slot * B + face_ref[r, 7]
            turn = (first - start + LANES) & (LANES - 1)
            base = face_ref[r, 0] * 128 + (side >> 1) * 64 + (side & 1) * 3
            lane = iota((RIM, LANES), 1)
            here = (lane >= first) & (lane < first + length)
            for j in range(3):
                values = rim_ref[pl.ds(base + j, planes, stride=RIM), :]
                values = jnp.where(here, pltpu.roll(values, turn, 1), 0.0)
                rows = pl.ds(target * FACE_ROWS + j * planes, planes)
                pay_ref[rows, :] = pay_ref[rows, :] + values
            rows = pl.ds(target * FACE_ROWS + 3 * planes, 1)
            pay_ref[rows, :] = pay_ref[rows, :] + jnp.where(here[:1], code, 0).astype(f32)

        return carry

    lax.fori_loop(0, face_ref.shape[0], face, 0)
    send = pltpu.make_async_copy(pay_ref, pay_hbm, sem)
    send.start()
    send.wait()


def depth_kernel(planes, table_ref, *refs):
    count = len(refs) // 2
    blocks, outs = refs[:count], refs[count:]
    total = count * planes
    t_hi, t_lo = split(table_ref[...])
    t_lo = jnp.where(iota((total, LANES), 1) < total, t_lo, jnp.zeros_like(t_lo))
    left = jnp.concatenate([t_hi, t_lo], 1)
    for q in range(4):
        right = jnp.concatenate(
            [
                jnp.concatenate(
                    [b[pl.ds(q * 8 + p, planes, stride=32), :] for b in blocks], 0
                )
                for p in range(8)
            ],
            1,
        )
        r_hi, r_lo = split(right)
        mixed = dot(left, jnp.concatenate([r_hi, r_lo, r_hi, r_lo], 0))
        for p in range(8):
            for s in range(count):
                outs[s][pl.ds(q * 8 + p, planes, stride=32), :] = mixed[
                    s * planes : (s + 1) * planes, p * LANES : (p + 1) * LANES
                ]


def advance_kernel(
    planes,
    total,
    mine_ref,
    box_ref,
    got_ref,
    rim_ref,
    now_hbm,
    prev_hbm,
    col_ref,
    row_ref,
    edge_row_ref,
    edge_col_ref,
    out_ref,
    sum_ref,
    times_ref,
    now_ref,
    prev_ref,
    label_ref,
    code_ref,
    even_down_ref,
    even_hi_ref,
    even_lo_ref,
    odd_down_ref,
    odd_hi_ref,
    odd_lo_ref,
    sems,
):
    holders = col_ref.shape[0]
    fetches = [
        pltpu.make_async_copy(now_hbm, now_ref, sems.at[0]),
        pltpu.make_async_copy(prev_hbm, prev_ref, sems.at[1]),
    ]
    for copy in fetches:
        copy.start()
    sources = got_ref.shape[0] // FACE_ROWS
    labels = got_ref[pl.ds(3 * planes, sources, stride=FACE_ROWS), :]
    place = iota((sources, LANES), 1)
    first = jnp.max(jnp.where(place < B, labels, 0.0), 1, keepdims=True)
    second = jnp.max(jnp.where(place < B, 0.0, labels), 1, keepdims=True)
    label_ref[...] = jnp.where(place == 0, first, second).astype(jnp.int32)
    to_scalars = pltpu.make_async_copy(label_ref, code_ref, sems.at[2])
    to_scalars.start()
    sum_ref[...] = jnp.zeros_like(sum_ref)
    times_ref[...] = jnp.zeros_like(times_ref)

    to_scalars.wait()

    def gather(k, carry):
        code = code_ref[k >> 1, k & 1]

        @pl.when(code > 0)
        def _():
            source = k >> 1
            turn = (k & 1) * B
            which = code - 1
            tile = which >> 1
            first = (which & 1) * 3
            base = source * FACE_ROWS
            marks = got_ref[pl.ds(base + 3 * planes, 1), :]
            marks = pltpu.roll(jnp.broadcast_to(marks, (RIM, LANES)), turn, 1)
            here = (marks == code.astype(f32)) & (iota((RIM, LANES), 1) < B)
            for j in range(3):
                values = got_ref[pl.ds(base + j * planes, planes), :]
                values = jnp.where(here, pltpu.roll(values, turn, 1), 0.0)
                rows = pl.ds(tile * 64 + first + j, planes, stride=RIM)
                sum_ref[rows, :] = sum_ref[rows, :] + values
            row = iota((RIM, LANES), 0)
            hit = here & (row >= first) & (row < first + 3)
            rows = pl.ds(pl.multiple_of(tile * RIM, RIM), RIM)
            times_ref[rows, :] = times_ref[rows, :] + jnp.where(hit, 1.0, 0.0)

        return carry

    lax.fori_loop(0, 2 * sources, gather, 0)
    first_plane = mine_ref[0] * planes
    lane = iota((32, LANES), 1)
    half = iota((RIM, LANES), 1) < B

    def faces(p, down_ref, right_hi_ref, right_lo_ref):
        jumps = []
        for axis in range(2):
            rows = pl.ds(pl.multiple_of((p * 2 + axis) * 64, 64), 64)
            times = times_ref[pl.ds(pl.multiple_of((p * 2 + axis) * RIM, RIM), RIM), :]
            times = jnp.concatenate([times] * planes, 0)
            jumps.append(split(sum_ref[rows, :] - times * rim_ref[rows, :]))
        j_hi, j_lo = jumps[0]
        c_hi, c_lo = split(jnp.concatenate([col_ref[p], jnp.zeros((B, LANES), f32)], 0))
        along_y = dot(
            jnp.concatenate([j_hi, j_hi, j_lo], 1), jnp.concatenate([c_hi, c_lo, c_hi], 0)
        )
        j_hi, j_lo = jumps[1]
        r_hi, r_lo = split(row_ref[p])
        along_x = lax.dot_general(
            jnp.concatenate([r_hi, r_lo, r_hi], 1),
            jnp.concatenate([j_hi, j_hi, j_lo], 1),
            (((1,), (1,)), ((), ())),
            preferred_element_type=f32,
        )
        down_ref[...] = jnp.concatenate([along_x[:32], along_x[32:]], 1)
        for kz in range(planes):
            tile = along_y[kz * RIM : (kz + 1) * RIM]
            both = jnp.concatenate([jnp.where(half, tile, 0.0), jnp.where(half, 0.0, tile)], 0)
            spot = slice(kz * 2 * RIM, (kz + 1) * 2 * RIM)
            right_hi_ref[spot], right_lo_ref[spot] = split(both)

    def finish(p, down_ref, right_hi_ref, right_lo_ref):
        edge_hi, edge_lo = split(edge_row_ref[p])
        down_hi, down_lo = split(down_ref[...])
        left_hi = []
        left_lo = []
        for kz in range(planes):
            near = jnp.where(lane // 16 == kz, 1.0, 0.0).astype(bf16)
            far = jnp.where((lane // RIM) % planes == kz, 1.0, 0.0).astype(bf16)
            left_hi.append(jnp.concatenate([edge_hi * near, down_hi * far], 1))
            left_lo.append(jnp.concatenate([edge_lo * near, down_lo * far], 1))
        left_hi = jnp.concatenate(left_hi, 0)
        left_lo = jnp.concatenate(left_lo, 0)
        edges = edge_col_ref[p]
        edges = jnp.concatenate([edges[:RIM]] * planes + [edges[RIM:]] * planes, 0)
        edges_hi, edges_lo = split(edges)
        right_hi = jnp.concatenate([right_hi_ref[...], edges_hi], 0)
        right_lo = jnp.concatenate([right_lo_ref[...], edges_lo], 0)
        force = dot(
            jnp.concatenate([left_hi, left_hi, left_lo], 1),
            jnp.concatenate([right_hi, right_lo, right_hi], 0),
        )
        ex = box_ref[p, 0]
        ey = box_ref[p, 1]
        wave_x = 2 * iota((32, LANES), 0) + lane // B
        wave_y = lane % B
        inside = (wave_x < ex) & (wave_y < ey)
        unit = TIME_STEP * np.pi
        scale_x = unit / jnp.full((1, LANES), ex, jnp.int32).astype(f32)
        scale_y = unit / jnp.full((1, LANES), ey, jnp.int32).astype(f32)
        flat = (wave_x.astype(f32) * scale_x) ** 2 + (wave_y.astype(f32) * scale_y) ** 2
        for kz in range(planes):
            depth = (first_plane + kz).astype(f32) * (unit / total)
            u = flat + depth * depth
            s = f32(WAVE[-1])
            for c in WAVE[-2::-1]:
                s = s * u + f32(c)
            rows = pl.ds(kz * 256 + p, 32, stride=8)
            new = (2.0 - u * s) * now_ref[rows, :] - prev_ref[rows, :]
            new = new + s * (force[kz * 32 : (kz + 1) * 32] * (TIME_STEP * TIME_STEP))
            out_ref[rows, :] = jnp.where(inside, new, 0.0)

    def two(i, carry):
        faces(2 * i, *even)
        finish(jnp.maximum(2 * i - 1, 0), *odd)
        faces(2 * i + 1, *odd)
        finish(2 * i, *even)
        return carry

    for copy in fetches:
        copy.wait()
    even = (even_down_ref, even_hi_ref, even_lo_ref)
    odd = (odd_down_ref, odd_hi_ref, odd_lo_ref)
    for ref in odd:
        ref[...] = jnp.zeros_like(ref)
    lax.fori_loop(0, holders // 2, two, 0)
    finish(holders - 1, *odd)


def join_kernel(mine_ref, *refs):
    count = (len(refs) - 2)
    blocks, out_ref, sems = refs[:count], refs[count], refs[count + 1]
    mine = mine_ref[0]
    copies = []
    for s, block in enumerate(blocks):
        spot = pl.multiple_of((mine ^ s) * 32, 32)
        copies.append(pltpu.make_async_copy(block, out_ref.at[:, pl.ds(spot, 32), :], sems.at[s]))
    for copy in copies:
        copy.start()
    for copy in copies:
        copy.wait()


HB = pl.BlockSpec(memory_space=pltpu.HBM)
VM = pl.BlockSpec(memory_space=pltpu.VMEM)
SM = pl.BlockSpec(memory_space=pltpu.SMEM)


def call(kernel, args, spots, outs, scratch=(), spot=VM):
    return pl.pallas_call(
        kernel,
        out_shape=outs,
        in_specs=spots,
        out_specs=tuple(spot) if isinstance(spot, list) else jax.tree.map(lambda _: spot, outs),
        scratch_shapes=list(scratch),
        compiler_params=pltpu.CompilerParams(vmem_limit_bytes=16 * 2**20),
        cost_estimate=pl.CostEstimate(flops=10**8, bytes_accessed=4 * 2**20, transcendentals=0),
    )(*args)


def swap(block, step):
    count = lax.axis_size("height")
    return lax.ppermute(block, "height", [(i, i ^ step) for i in range(count)])


def tiles(field):
    planes, holders, cells = field.shape
    split_up = field.reshape(planes, holders, cells // LANES, LANES).transpose(0, 2, 1, 3)
    return split_up.reshape(-1, LANES)


def untiles(rows, planes, holders):
    cells = rows.shape[0] // (planes * holders)
    folded = rows.reshape(planes, cells, holders, LANES).transpose(0, 2, 1, 3)
    return folded.reshape(planes, holders, cells * LANES)


def step(modes_now, modes_prev, partition_boxes, face_table):
    planes, holders, _ = modes_now.shape
    count = lax.axis_size("height")
    domains = lax.axis_size("dom")
    total = planes * count
    mine = lax.axis_index("height").astype(jnp.int32)
    extent_rows = partition_boxes[:, 0]
    extent_cols = partition_boxes[:, 1]
    now = pltpu.with_memory_space_constraint(tiles(modes_now), pltpu.HBM)
    prev = pltpu.with_memory_space_constraint(tiles(modes_prev), pltpu.HBM)
    mine_word = mine.reshape(1)

    def rows(n):
        return jax.ShapeDtypeStruct((n, LANES), f32)

    pieces, rim = call(
        functools.partial(cells_kernel, planes),
        (mine_word, partition_boxes, now),
        [SM, SM, HB],
        (rows(2048), rows(holders * 128)),
        [
            pltpu.VMEM((2048, LANES), f32),
            pltpu.VMEM((holders * B, LANES), f32),
            pltpu.VMEM((holders, LANES, 2 * LANES), bf16),
            pltpu.VMEM((holders, LANES, 2 * LANES), bf16),
            pltpu.VMEM((holders, 144, LANES), bf16),
            pltpu.VMEM((holders, 144, LANES), bf16),
            pltpu.VMEM((B, (planes + 1) * LANES), bf16),
            pltpu.VMEM((B, (planes + 1) * LANES), bf16),
            pltpu.VMEM((B, (planes + 1) * LANES), bf16),
            pltpu.VMEM((B, (planes + 1) * LANES), bf16),
            pltpu.SemaphoreType.DMA,
        ],
    )
    pay = call(
        functools.partial(pack_kernel, planes),
        (face_table, rim),
        [SM, VM],
        rows(domains * FACE_ROWS),
        [
            pltpu.SMEM((domains,), jnp.int32),
            pltpu.VMEM((domains * FACE_ROWS, LANES), f32),
            pltpu.SemaphoreType.DMA,
        ],
        spot=HB,
    )
    pieces = pieces.reshape(count, 256, LANES)
    got = [pieces[0]] + [swap(pieces[s], s) for s in range(1, count)]
    arrived = lax.all_to_all(pay.reshape(-1, 1, LANES), "dom", 0, 0, tiled=True)

    order = (mine ^ jnp.arange(count, dtype=jnp.int32))[:, None] * planes
    order = (order + jnp.arange(planes, dtype=jnp.int32)).reshape(-1)
    depth_table = cosine(jnp.full((), total, jnp.int32), order[None, :], order[:, None])
    depth_table = jnp.concatenate([depth_table, depth_table], 1)
    mixed = call(
        functools.partial(depth_kernel, planes),
        (depth_table, *got),
        [VM] * (1 + count),
        (rows(256),) * count,
    )
    back = [mixed[0]] + [swap(mixed[s], s) for s in range(1, count)]

    new = call(
        functools.partial(advance_kernel, planes, total),
        (mine_word, partition_boxes, arrived.reshape(-1, LANES), rim, now, prev)
        + tuple(backward_tables(extent_rows, extent_cols)),
        [SM] * 2 + [VM] * 2 + [HB] * 2 + [VM] * 4,
        rows(2048),
        [
            pltpu.VMEM((holders * 128, LANES), f32),
            pltpu.VMEM((holders * 2 * RIM, LANES), f32),
            pltpu.VMEM((2048, LANES), f32),
            pltpu.VMEM((2048, LANES), f32),
            pltpu.VMEM((domains, LANES), jnp.int32),
            pltpu.SMEM((domains, LANES), jnp.int32),
        ]
        + [
            pltpu.VMEM((32, LANES), f32),
            pltpu.VMEM((LANES, LANES), bf16),
            pltpu.VMEM((LANES, LANES), bf16),
        ]
        * 2
        + [pltpu.SemaphoreType.DMA((3,))],
    )
    pressure = call(
        join_kernel,
        (mine_word, *[b.reshape(planes, 32, LANES) for b in back]),
        [SM] + [VM] * count,
        jax.ShapeDtypeStruct((planes, 256, LANES), f32),
        [pltpu.SemaphoreType.DMA((count,))],
        spot=HB,
    )
    pressure = untiles(pressure.reshape(-1, LANES), planes, holders)
    return untiles(new, planes, holders), pressure


def solution(mesh):
    placed = (P("height", "dom", None), P("height", "dom", None), P("dom", None), P("dom", None))
    return jax.shard_map(
        step,
        mesh=mesh,
        in_specs=placed,
        out_specs=(P("height", "dom", None), P("height", "dom", None)),
        check_vma=False,
    )
```

```python
import functools

import jax
import jax.numpy as jnp
import numpy as np
from jax import lax
from jax.experimental import pallas as pl
from jax.experimental.pallas import tpu as pltpu
from jax.sharding import PartitionSpec as P


B = 64
LANES = 128
FACE_ROWS = 25
RIM = 8

COUPLING = 32.0
STENCIL = (COUPLING * 270.0 / 180.0, COUPLING * -27.0 / 180.0, COUPLING * 2.0 / 180.0)
TIME_STEP = 0.4
WAVE = (
    0.9999999998806415,
    -0.08333333151883045,
    0.002777773302928117,
    -4.959913250130888e-05,
    5.494915434656933e-07,
    -3.861085658928547e-09,
)


bf16 = jnp.bfloat16
f32 = jnp.float32


def cosine(length, wave, place):
    angle = wave * (2 * place + 1)
    period = 4 * length
    turns = jnp.floor((angle.astype(f32) + 0.5) / period.astype(f32)).astype(jnp.int32)
    angle = angle - turns * period
    angle = jnp.minimum(angle, period - angle)
    x = (length - angle).astype(f32) * ((np.pi / 2) / length.astype(f32))
    y = x * x
    s = f32(-2.50521084e-8)
    for c in (2.75573192e-6, -1.98412698e-4, 8.33333333e-3, -1.66666667e-1):
        s = s * y + f32(c)
    s = x + x * y * s
    scale = jnp.sqrt(jnp.where(wave == 0, 1.0, 2.0) / length.astype(f32))
    inside = (wave < length) & (place < length) & (place >= 0)
    return jnp.where(inside, scale * s, 0.0)


def iota(shape, axis):
    return lax.broadcasted_iota(jnp.int32, shape, axis)


def rim_cell(index, extent):
    return jnp.where(index < 3, index, jnp.where(index < 6, extent + 2 - index, -1))


def split(x):
    hi = x.astype(bf16)
    lo = (x - hi.astype(f32)).astype(bf16)
    return hi, lo


def dot(a, b):
    return jnp.dot(a, b, preferred_element_type=f32)


def cosine_tile(length, wave, place):
    size = jnp.full((1, LANES), length, jnp.int32).astype(f32)
    unit = 1.0 / size
    angle = wave * (2.0 * place + 1.0)
    angle = angle - jnp.floor((angle + 0.5) * (0.25 * unit)) * (4.0 * size)
    angle = jnp.minimum(angle, 4.0 * size - angle)
    x = (size - angle) * (f32(np.pi / 2) * unit)
    y = x * x
    s = f32(-2.50521084e-8)
    for c in (2.75573192e-6, -1.98412698e-4, 8.33333333e-3, -1.66666667e-1):
        s = s * y + f32(c)
    s = x + x * y * s
    s = s * jnp.where(wave == 0.0, jnp.sqrt(unit), jnp.sqrt(2.0 * unit))
    return jnp.where((wave < size) & (place < size) & (place >= 0.0), s, 0.0)


def cells_kernel(
    planes,
    mine_ref,
    box_ref,
    x_hbm,
    even_ref,
    odd_ref,
    rim_ref,
    x_ref,
    stage0_ref,
    stage1_ref,
    table_ref,
    c_hi_ref,
    c_lo_ref,
    l_hi_ref,
    l_lo_ref,
    even_hi_ref,
    even_lo_ref,
    odd_hi_ref,
    odd_lo_ref,
    sem,
):
    mine = mine_ref[0]
    holders = box_ref.shape[1]
    fetch = pltpu.make_async_copy(x_hbm, x_ref, sem)
    fetch.start()
    low32 = iota((32, LANES), 1) < B
    low8 = iota((8, LANES), 1) < B
    lane = iota((B, LANES), 1)
    low = lane < B
    row64 = iota((B, LANES), 0).astype(f32)
    x_wave = 2 * (lane % 32) + (lane // 32) % 2
    x_wave64 = x_wave.astype(f32)
    x_wave8 = x_wave[:8].astype(f32)
    l_low = iota((144, LANES), 1) < B

    def tables(p, carry):
        ex = box_ref[0, p]
        ey = box_ref[1, p]
        c = cosine_tile(ey, row64, jnp.where(low, lane, rim_cell(lane - B, ey)).astype(f32))
        turned = pltpu.roll(c, B, 1)
        c = jnp.concatenate(
            [
                jnp.concatenate([jnp.where(low, c, 0.0), jnp.where(low, turned, 0.0)], 1),
                jnp.concatenate([jnp.where(low, 0.0, turned), jnp.where(low, 0.0, c)], 1),
            ],
            0,
        )
        c_hi_ref[p], c_lo_ref[p] = split(c)
        spot = pl.multiple_of(p * B, B)
        g = cosine_tile(ex, x_wave64, row64)
        table_ref[pl.ds(spot, B), :] = g
        edge = cosine_tile(ex, x_wave8, rim_cell(iota((8, LANES), 0), ex).astype(f32))
        rows = jnp.concatenate(
            [
                table_ref[pl.ds(spot, 32, stride=2), :],
                pltpu.roll(table_ref[pl.ds(spot + 1, 32, stride=2), :], 32, 1),
                edge,
                jnp.zeros((8, LANES), f32),
                g,
            ],
            0,
        )
        l_hi, l_lo = split(rows)
        l_hi_ref[p] = l_hi
        l_lo_ref[p] = jnp.where(l_low, l_lo, jnp.zeros_like(l_lo))
        return carry

    lax.fori_loop(0, holders, tables, 0)
    fetch.wait()

    def along_y(p, r_hi_ref, r_lo_ref):
        x = jnp.concatenate(
            [x_ref[pl.ds(kz * 256 + p, 32, stride=8), :] for kz in range(planes)], 0
        )
        c_hi, c_lo = c_hi_ref[p], c_lo_ref[p]
        x_hi, x_lo = split(x)
        t = dot(
            jnp.concatenate([x_hi, x_hi, x_lo], 1), jnp.concatenate([c_hi, c_lo, c_hi], 0)
        )
        main = [t[kz * 32 : (kz + 1) * 32, :LANES] for kz in range(planes)]
        rims = t[0:32, LANES:]
        for kz in range(1, planes):
            rims = rims + pltpu.roll(t[kz * 32 : (kz + 1) * 32, LANES:], kz * RIM, 1)
        main.append(rims)
        for i, part in enumerate(main):
            hi, lo = split(jnp.concatenate([part, pltpu.roll(part, B, 1)], 0))
            r_hi_ref[:, i * LANES : (i + 1) * LANES] = hi
            r_lo_ref[:, i * LANES : (i + 1) * LANES] = lo

    def along_x(p, r_hi_ref, r_lo_ref, stage_ref):
        r_hi, r_lo = r_hi_ref[...], r_lo_ref[...]
        right = jnp.concatenate([r_hi, r_lo, r_hi, r_lo], 0)
        left = jnp.concatenate([l_hi_ref[p], l_lo_ref[p]], 1)
        y = dot(left[:80], right[:, : planes * LANES])
        z = dot(left[80:], right[:, planes * LANES :])
        for kz in range(planes):
            tile = y[:, kz * LANES : (kz + 1) * LANES]
            out = jnp.where(low32, tile[:32], tile[32:64])
            stage_ref[kz * 32 : (kz + 1) * 32, :] = out
            for s in range(8):
                spot = (s // 2) * 256 + kz * 32 + p
                (even_ref, odd_ref)[s % 2][pl.ds(spot, 4, stride=8), :] = stage_ref[
                    pl.ds(kz * 32 + (mine ^ s) * 4, 4), :
                ]
            rim_ref[pl.ds(pl.multiple_of(p * 128 + kz * RIM, RIM), RIM), :] = jnp.where(
                low8, tile[64:72], 0.0
            )
        rim_ref[pl.ds(pl.multiple_of(p * 128 + 64, 64), 64), :] = jnp.concatenate(
            [z.T[:64], jnp.zeros((64, 64), f32)], 1
        )

    even = (even_hi_ref, even_lo_ref)
    odd = (odd_hi_ref, odd_lo_ref)

    def two(i, carry):
        along_y(2 * i, *even)
        along_x(jnp.maximum(2 * i - 1, 0), *odd, stage1_ref)
        along_y(2 * i + 1, *odd)
        along_x(2 * i, *even, stage0_ref)
        return carry

    lax.fori_loop(0, holders // 2, two, 0)
    along_x(holders - 1, *odd, stage1_ref)


def pack_kernel(planes, face_ref, rim_ref, pay_hbm, rim_hbm, used_ref, pay_ref, sems):
    keep = pltpu.make_async_copy(rim_ref, rim_hbm, sems.at[0])
    keep.start()
    pay_ref[...] = jnp.zeros_like(pay_ref)
    targets = pay_ref.shape[0] // FACE_ROWS

    def clear(t, carry):
        used_ref[t] = 0
        return carry

    lax.fori_loop(0, targets, clear, 0)

    lane = iota((planes, LANES), 1)

    def face(r, carry):
        length = face_ref[3, r]
        live = (length > 0).astype(jnp.int32)
        side = face_ref[1, r]
        target = face_ref[4, r] * live
        code = face_ref[5, r] * 4 + face_ref[6, r] + 1
        slot = used_ref[target] * live
        used_ref[target] = used_ref[target] + live
        first = slot * B + face_ref[7, r]
        turn = (first - face_ref[2, r] + LANES) & (LANES - 1)
        base = face_ref[0, r] * 128 + (side >> 1) * 64 + (side & 1) * 3
        here = (lane >= first) & (lane < first + length)
        for j in range(3):
            values = pltpu.roll(rim_ref[pl.ds(base + j, planes, stride=RIM), :], turn, 1)
            rows = pl.ds(target * FACE_ROWS + j * planes, planes)
            pltpu.store(pay_ref.at[rows, :], values, mask=here)
        rows = pl.ds(target * FACE_ROWS + 3 * planes, 1)
        label = jnp.full((1, LANES), code, jnp.int32).astype(f32)
        pltpu.store(pay_ref.at[rows, :], label, mask=here[:1])
        return carry

    lax.fori_loop(0, face_ref.shape[1], face, 0, unroll=4)
    send = pltpu.make_async_copy(pay_ref, pay_hbm, sems.at[1])
    send.start()
    keep.wait()
    send.wait()


def depth_kernel(planes, table_ref, own_ref, near_ref, *refs):
    far, outs = refs[:-2], refs[-2:]
    count = 2 + 2 * len(far)
    size = 32 * planes
    blocks = [(own_ref, 0), (near_ref, 0)] + [(r, i * size) for r in far for i in range(2)]
    total = count * planes
    t_hi, t_lo = split(table_ref[...])
    t_lo = jnp.where(iota((total, LANES), 1) < total, t_lo, jnp.zeros_like(t_lo))
    left = jnp.concatenate([t_hi, t_lo], 1)
    for q in range(4):
        right = jnp.concatenate(
            [
                jnp.concatenate(
                    [b[pl.ds(at + q * 8 + p, planes, stride=32), :] for b, at in blocks], 0
                )
                for p in range(8)
            ],
            1,
        )
        r_hi, r_lo = split(right)
        mixed = dot(left, jnp.concatenate([r_hi, r_lo, r_hi, r_lo], 0))
        for p in range(8):
            for s in range(count):
                spot = (s // 2) * size + q * 8 + p
                outs[s % 2][pl.ds(spot, planes, stride=32), :] = mixed[
                    s * planes : (s + 1) * planes, p * LANES : (p + 1) * LANES
                ]


def advance_kernel(
    planes,
    total,
    mine_ref,
    box_ref,
    got_ref,
    rim_hbm,
    now_hbm,
    prev_hbm,
    col_hbm,
    row_hbm,
    edge_row_hbm,
    edge_col_hbm,
    out_ref,
    sum_ref,
    times_ref,
    now_ref,
    prev_ref,
    rim_ref,
    col_ref,
    row_ref,
    edge_row_ref,
    edge_col_ref,
    label_ref,
    code_ref,
    even_down_ref,
    even_hi_ref,
    even_lo_ref,
    odd_down_ref,
    odd_hi_ref,
    odd_lo_ref,
    sems,
):
    holders = col_hbm.shape[0]
    fetches = [
        pltpu.make_async_copy(rim_hbm, rim_ref, sems.at[0]),
        pltpu.make_async_copy(col_hbm, col_ref, sems.at[1]),
        pltpu.make_async_copy(row_hbm, row_ref, sems.at[2]),
        pltpu.make_async_copy(edge_row_hbm, edge_row_ref, sems.at[3]),
        pltpu.make_async_copy(edge_col_hbm, edge_col_ref, sems.at[4]),
        pltpu.make_async_copy(now_hbm, now_ref, sems.at[5]),
        pltpu.make_async_copy(prev_hbm, prev_ref, sems.at[6]),
    ]
    for copy in fetches:
        copy.start()
    sources = got_ref.shape[0] // FACE_ROWS
    labels = got_ref[pl.ds(3 * planes, sources, stride=FACE_ROWS), :]
    place = iota((sources, LANES), 1)
    first = jnp.max(jnp.where(place < B, labels, 0.0), 1, keepdims=True)
    second = jnp.max(jnp.where(place < B, 0.0, labels), 1, keepdims=True)
    label_ref[...] = jnp.where(place == 0, first, second).astype(jnp.int32)
    to_scalars = pltpu.make_async_copy(label_ref, code_ref, sems.at[7])
    to_scalars.start()
    sum_ref[...] = jnp.zeros_like(sum_ref)
    times_ref[...] = jnp.zeros_like(times_ref)

    to_scalars.wait()

    def gather(k, carry):
        code = code_ref[k >> 1, k & 1]

        @pl.when(code > 0)
        def _():
            source = k >> 1
            turn = (k & 1) * B
            which = code - 1
            tile = which >> 1
            first = (which & 1) * 3
            base = source * FACE_ROWS
            marks = got_ref[pl.ds(base + 3 * planes, 1), :]
            marks = pltpu.roll(jnp.broadcast_to(marks, (RIM, LANES)), turn, 1)
            here = (marks == code.astype(f32)) & (iota((RIM, LANES), 1) < B)
            for j in range(3):
                values = got_ref[pl.ds(base + j * planes, planes), :]
                values = jnp.where(here, pltpu.roll(values, turn, 1), 0.0)
                rows = pl.ds(tile * 64 + first + j, planes, stride=RIM)
                sum_ref[rows, :] = sum_ref[rows, :] + values
            row = iota((RIM, LANES), 0)
            hit = here & (row >= first) & (row < first + 3)
            rows = pl.ds(pl.multiple_of(tile * RIM, RIM), RIM)
            times_ref[rows, :] = times_ref[rows, :] + jnp.where(hit, 1.0, 0.0)

        return carry

    lax.fori_loop(0, 2 * sources, gather, 0)
    first_plane = mine_ref[0] * planes
    lane = iota((32, LANES), 1)
    half = iota((RIM, LANES), 1) < B

    def faces(p, down_ref, right_hi_ref, right_lo_ref):
        jumps = []
        for axis in range(2):
            rows = pl.ds(pl.multiple_of((p * 2 + axis) * 64, 64), 64)
            times = times_ref[pl.ds(pl.multiple_of((p * 2 + axis) * RIM, RIM), RIM), :]
            times = jnp.concatenate([times] * planes, 0)
            jumps.append(split(sum_ref[rows, :] - times * rim_ref[rows, :]))
        j_hi, j_lo = jumps[0]
        c_hi, c_lo = split(jnp.concatenate([col_ref[p], jnp.zeros((B, LANES), f32)], 0))
        along_y = dot(
            jnp.concatenate([j_hi, j_hi, j_lo], 1), jnp.concatenate([c_hi, c_lo, c_hi], 0)
        )
        j_hi, j_lo = jumps[1]
        r_hi, r_lo = split(row_ref[p])
        along_x = lax.dot_general(
            jnp.concatenate([r_hi, r_lo, r_hi], 1),
            jnp.concatenate([j_hi, j_hi, j_lo], 1),
            (((1,), (1,)), ((), ())),
            preferred_element_type=f32,
        )
        down_ref[...] = jnp.concatenate([along_x[:32], along_x[32:]], 1)
        for kz in range(planes):
            tile = along_y[kz * RIM : (kz + 1) * RIM]
            both = jnp.concatenate([jnp.where(half, tile, 0.0), jnp.where(half, 0.0, tile)], 0)
            spot = slice(kz * 2 * RIM, (kz + 1) * 2 * RIM)
            right_hi_ref[spot], right_lo_ref[spot] = split(both)

    def finish(p, down_ref, right_hi_ref, right_lo_ref):
        edge_hi, edge_lo = split(edge_row_ref[p])
        down_hi, down_lo = split(down_ref[...])
        left_hi = []
        left_lo = []
        for kz in range(planes):
            near = jnp.where(lane // 16 == kz, 1.0, 0.0).astype(bf16)
            far = jnp.where((lane // RIM) % planes == kz, 1.0, 0.0).astype(bf16)
            left_hi.append(jnp.concatenate([edge_hi * near, down_hi * far], 1))
            left_lo.append(jnp.concatenate([edge_lo * near, down_lo * far], 1))
        left_hi = jnp.concatenate(left_hi, 0)
        left_lo = jnp.concatenate(left_lo, 0)
        edges = edge_col_ref[p]
        edges = jnp.concatenate([edges[:RIM]] * planes + [edges[RIM:]] * planes, 0)
        edges_hi, edges_lo = split(edges)
        right_hi = jnp.concatenate([right_hi_ref[...], edges_hi], 0)
        right_lo = jnp.concatenate([right_lo_ref[...], edges_lo], 0)
        force = dot(
            jnp.concatenate([left_hi, left_hi, left_lo], 1),
            jnp.concatenate([right_hi, right_lo, right_hi], 0),
        )
        ex = box_ref[0, p]
        ey = box_ref[1, p]
        wave_x = 2 * iota((32, LANES), 0) + lane // B
        wave_y = lane % B
        inside = (wave_x < ex) & (wave_y < ey)
        unit = TIME_STEP * np.pi
        scale_x = unit / jnp.full((1, LANES), ex, jnp.int32).astype(f32)
        scale_y = unit / jnp.full((1, LANES), ey, jnp.int32).astype(f32)
        flat = (wave_x.astype(f32) * scale_x) ** 2 + (wave_y.astype(f32) * scale_y) ** 2
        for kz in range(planes):
            depth = (first_plane + kz).astype(f32) * (unit / total)
            u = flat + depth * depth
            s = f32(WAVE[-1])
            for c in WAVE[-2::-1]:
                s = s * u + f32(c)
            rows = pl.ds(kz * 256 + p, 32, stride=8)
            new = (2.0 - u * s) * now_ref[rows, :] - prev_ref[rows, :]
            new = new + s * (force[kz * 32 : (kz + 1) * 32] * (TIME_STEP * TIME_STEP))
            out_ref[rows, :] = jnp.where(inside, new, 0.0)

    def two(i, carry):
        faces(2 * i, *even)
        finish(jnp.maximum(2 * i - 1, 0), *odd)
        faces(2 * i + 1, *odd)
        finish(2 * i, *even)
        return carry

    for copy in fetches:
        copy.wait()
    even = (even_down_ref, even_hi_ref, even_lo_ref)
    odd = (odd_down_ref, odd_hi_ref, odd_lo_ref)
    for ref in odd:
        ref[...] = jnp.zeros_like(ref)
    lax.fori_loop(0, holders // 2, two, 0)
    finish(holders - 1, *odd)


def tables_kernel(box_ref, *refs):
    outs, held, sems = refs[:4], refs[4:8], refs[8]
    col_ref, row_ref, edge_row_ref, edge_col_ref = held
    down = iota((B, LANES), 0)
    lane = iota((B, LANES), 1)
    col_wave = (lane % B).astype(f32)
    row_wave = (2 * (down % 32) + down // 32).astype(f32)
    across = lane.astype(f32)
    below = down.astype(f32)
    low = lane < B

    def weights(index):
        layer = index % 3
        table = [jnp.zeros(index.shape, f32)] * 3
        for i in range(3):
            for j in range(3 - i):
                table[i] = jnp.where((layer == j) & (index < 6), STENCIL[i + j], table[i])
        return table

    row_lane = lane[:32]
    row_index = row_lane % 8
    row_weights = weights(row_index)
    edge_row_wave = (2 * down[:32] + (row_lane // 8) % 2).astype(f32)
    col_index = down[:16] % 8
    col_mine = down[:16] // 8 == lane[:16] // B
    col_weights = [jnp.where(col_mine, w, 0.0) for w in weights(col_index)]
    edge_col_wave = col_wave[:16]

    def one(p, carry):
        ex = box_ref[0, p]
        ey = box_ref[1, p]
        col_ref[p] = cosine_tile(ey, col_wave, below)
        row_ref[p] = jnp.where(low, cosine_tile(ex, row_wave, across), 0.0)
        for extent, wave, index, weight, ref in (
            (ex, edge_row_wave, row_index, row_weights, edge_row_ref),
            (ey, edge_col_wave, col_index, col_weights, edge_col_ref),
        ):
            total = jnp.zeros(wave.shape, f32)
            for i in range(3):
                cell = jnp.where(index < 3, i, extent - 1 - i).astype(f32)
                total = total + weight[i] * cosine_tile(extent, wave, cell)
            ref[p] = total
        return carry

    lax.fori_loop(0, box_ref.shape[1], one, 0, unroll=2)
    copies = [pltpu.make_async_copy(h, o, sems.at[i]) for i, (h, o) in enumerate(zip(held, outs))]
    for copy in copies:
        copy.start()
    for copy in copies:
        copy.wait()


def join_kernel(planes, mine_ref, own_ref, near_ref, *refs):
    far, out_ref, sems = refs[:-2], refs[-2], refs[-1]
    mine = mine_ref[0]
    blocks = [own_ref.at[:planes], near_ref.at[:planes]]
    blocks += [r.at[pl.ds(i * planes, planes)] for r in far for i in range(2)]
    copies = []
    for s, block in enumerate(blocks):
        spot = pl.multiple_of((mine ^ s) * 32, 32)
        copies.append(pltpu.make_async_copy(block, out_ref.at[:, pl.ds(spot, 32), :], sems.at[s]))
    for copy in copies:
        copy.start()
    for copy in copies:
        copy.wait()


HB = pl.BlockSpec(memory_space=pltpu.HBM)
VM = pl.BlockSpec(memory_space=pltpu.VMEM)
SM = pl.BlockSpec(memory_space=pltpu.SMEM)


def call(kernel, args, spots, outs, scratch=(), spot=VM):
    return pl.pallas_call(
        kernel,
        out_shape=outs,
        in_specs=spots,
        out_specs=tuple(spot) if isinstance(spot, list) else jax.tree.map(lambda _: spot, outs),
        scratch_shapes=list(scratch),
        compiler_params=pltpu.CompilerParams(vmem_limit_bytes=16 * 2**20),
        cost_estimate=pl.CostEstimate(flops=10**8, bytes_accessed=4 * 2**20, transcendentals=0),
    )(*args)


def swap(block, step):
    count = lax.axis_size("height")
    return lax.ppermute(block, "height", [(i, i ^ step) for i in range(count)])


def across(blocks, near):
    size = blocks.shape[0] // 4
    return [
        swap(
            jnp.concatenate(
                [blocks[t * size : (t + 1) * size], near[t * size : (t + 1) * size]], 0
            ),
            2 * t,
        )
        for t in range(1, 4)
    ]


def in_hbm(x):
    return pltpu.with_memory_space_constraint(x, pltpu.HBM)


def tiles(field):
    planes, holders, cells = field.shape
    split_up = field.reshape(planes, holders, cells // LANES, LANES).transpose(0, 2, 1, 3)
    return split_up.reshape(-1, LANES)


def untiles(rows, planes, holders):
    cells = rows.shape[0] // (planes * holders)
    folded = rows.reshape(planes, cells, holders, LANES).transpose(0, 2, 1, 3)
    return folded.reshape(planes, holders, cells * LANES)


def step(modes_now, modes_prev, partition_boxes, face_table):
    planes, holders, _ = modes_now.shape
    count = lax.axis_size("height")
    domains = lax.axis_size("dom")
    total = planes * count
    mine = lax.axis_index("height").astype(jnp.int32)
    now = in_hbm(tiles(modes_now))
    prev = in_hbm(tiles(modes_prev))
    mine_word = mine.reshape(1)
    boxes = in_hbm(partition_boxes.T)
    face_rows = in_hbm(face_table.T)

    def rows(n):
        return jax.ShapeDtypeStruct((n, LANES), f32)

    half = 1024
    even, odd, rim = call(
        functools.partial(cells_kernel, planes),
        (mine_word, boxes, now),
        [SM, SM, HB],
        (rows(half), rows(half), rows(holders * 128)),
        [
            pltpu.VMEM((2048, LANES), f32),
            pltpu.VMEM((32 * planes, LANES), f32),
            pltpu.VMEM((32 * planes, LANES), f32),
            pltpu.VMEM((holders * B, LANES), f32),
            pltpu.VMEM((holders, LANES, 2 * LANES), bf16),
            pltpu.VMEM((holders, LANES, 2 * LANES), bf16),
            pltpu.VMEM((holders, 144, LANES), bf16),
            pltpu.VMEM((holders, 144, LANES), bf16),
            pltpu.VMEM((B, (planes + 1) * LANES), bf16),
            pltpu.VMEM((B, (planes + 1) * LANES), bf16),
            pltpu.VMEM((B, (planes + 1) * LANES), bf16),
            pltpu.VMEM((B, (planes + 1) * LANES), bf16),
            pltpu.SemaphoreType.DMA,
        ],
    )
    pay, rim = call(
        functools.partial(pack_kernel, planes),
        (face_rows, rim),
        [SM, VM],
        (rows(domains * FACE_ROWS), pltpu.HBM((holders * 128, LANES), f32)),
        [
            pltpu.SMEM((domains,), jnp.int32),
            pltpu.VMEM((domains * FACE_ROWS, LANES), f32),
            pltpu.SemaphoreType.DMA((2,)),
        ],
        spot=HB,
    )
    near = swap(odd, 1)
    far = across(even, near)
    arrived = lax.all_to_all(pay.reshape(-1, 1, LANES), "dom", 0, 0, tiled=True)

    order = (mine ^ jnp.arange(count, dtype=jnp.int32))[:, None] * planes
    order = (order + jnp.arange(planes, dtype=jnp.int32)).reshape(-1)
    depth_table = cosine(jnp.full((), total, jnp.int32), order[None, :], order[:, None])
    depth_table = jnp.concatenate([depth_table, depth_table], 1)
    mixed = call(
        functools.partial(depth_kernel, planes),
        (depth_table, even, near, *far),
        [VM] * (3 + len(far)),
        (rows(half),) * 2,
    )
    back_near = swap(mixed[1], 1)
    back_far = across(mixed[0], back_near)

    later, _ = lax.optimization_barrier((boxes, mixed[0]))
    tables = call(
        tables_kernel,
        (later,),
        [SM],
        tuple(
            pltpu.HBM((holders, n, LANES), f32) for n in (B, B, 32, 2 * RIM)
        ),
        [
            pltpu.VMEM((holders, B, LANES), f32),
            pltpu.VMEM((holders, B, LANES), f32),
            pltpu.VMEM((holders, 32, LANES), f32),
            pltpu.VMEM((holders, 2 * RIM, LANES), f32),
            pltpu.SemaphoreType.DMA((4,)),
        ],
        spot=HB,
    )
    new = call(
        functools.partial(advance_kernel, planes, total),
        (mine_word, boxes, arrived.reshape(-1, LANES), in_hbm(rim), now, prev)
        + tuple(in_hbm(t) for t in tables),
        [SM] * 2 + [VM] + [HB] * 7,
        rows(2048),
        [
            pltpu.VMEM((holders * 128, LANES), f32),
            pltpu.VMEM((holders * 2 * RIM, LANES), f32),
            pltpu.VMEM((2048, LANES), f32),
            pltpu.VMEM((2048, LANES), f32),
            pltpu.VMEM((holders * 128, LANES), f32),
            pltpu.VMEM((holders, B, LANES), f32),
            pltpu.VMEM((holders, B, LANES), f32),
            pltpu.VMEM((holders, 32, LANES), f32),
            pltpu.VMEM((holders, 16, LANES), f32),
            pltpu.VMEM((domains, LANES), jnp.int32),
            pltpu.SMEM((domains, LANES), jnp.int32),
        ]
        + [
            pltpu.VMEM((32, LANES), f32),
            pltpu.VMEM((LANES, LANES), bf16),
            pltpu.VMEM((LANES, LANES), bf16),
        ]
        * 2
        + [pltpu.SemaphoreType.DMA((8,))],
    )
    pressure = call(
        functools.partial(join_kernel, planes),
        (mine_word, *[b.reshape(-1, 32, LANES) for b in (mixed[0], back_near, *back_far)]),
        [SM] + [VM] * (2 + len(back_far)),
        jax.ShapeDtypeStruct((planes, 256, LANES), f32),
        [pltpu.SemaphoreType.DMA((count,))],
        spot=HB,
    )
    pressure = untiles(pressure.reshape(-1, LANES), planes, holders)
    return untiles(new, planes, holders), pressure


def solution(mesh):
    placed = (P("height", "dom", None), P("height", "dom", None), P("dom", None), P("dom", None))
    return jax.shard_map(
        step,
        mesh=mesh,
        in_specs=placed,
        out_specs=(P("height", "dom", None), P("height", "dom", None)),
        check_vma=False,
    )
```

```python
import functools

import jax
import jax.numpy as jnp
import numpy as np
from jax import lax
from jax.experimental import pallas as pl
from jax.experimental.pallas import tpu as pltpu
from jax.sharding import PartitionSpec as P


B = 64
LANES = 128
FACE_ROWS = 25
RIM = 8

COUPLING = 32.0
STENCIL = (COUPLING * 270.0 / 180.0, COUPLING * -27.0 / 180.0, COUPLING * 2.0 / 180.0)
TIME_STEP = 0.4
WAVE = (
    0.9999999998806415,
    -0.08333333151883045,
    0.002777773302928117,
    -4.959913250130888e-05,
    5.494915434656933e-07,
    -3.861085658928547e-09,
)


bf16 = jnp.bfloat16
f32 = jnp.float32


def cosine(length, wave, place):
    angle = wave * (2 * place + 1)
    period = 4 * length
    turns = jnp.floor((angle.astype(f32) + 0.5) / period.astype(f32)).astype(jnp.int32)
    angle = angle - turns * period
    angle = jnp.minimum(angle, period - angle)
    x = (length - angle).astype(f32) * ((np.pi / 2) / length.astype(f32))
    y = x * x
    s = f32(-2.50521084e-8)
    for c in (2.75573192e-6, -1.98412698e-4, 8.33333333e-3, -1.66666667e-1):
        s = s * y + f32(c)
    s = x + x * y * s
    scale = jnp.sqrt(jnp.where(wave == 0, 1.0, 2.0) / length.astype(f32))
    inside = (wave < length) & (place < length) & (place >= 0)
    return jnp.where(inside, scale * s, 0.0)


def iota(shape, axis):
    return lax.broadcasted_iota(jnp.int32, shape, axis)


def rim_cell(index, extent):
    return jnp.where(index < 3, index, jnp.where(index < 6, extent + 2 - index, -1))


def split(x):
    hi = x.astype(bf16)
    lo = (x - hi.astype(f32)).astype(bf16)
    return hi, lo


def dot(a, b):
    return jnp.dot(a, b, preferred_element_type=f32)


def cosine_tile(length, wave, place):
    size = jnp.full((1, LANES), length, jnp.int32).astype(f32)
    unit = 1.0 / size
    angle = wave * (2.0 * place + 1.0)
    angle = angle - jnp.floor((angle + 0.5) * (0.25 * unit)) * (4.0 * size)
    angle = jnp.minimum(angle, 4.0 * size - angle)
    x = (size - angle) * (f32(np.pi / 2) * unit)
    y = x * x
    s = f32(-2.50521084e-8)
    for c in (2.75573192e-6, -1.98412698e-4, 8.33333333e-3, -1.66666667e-1):
        s = s * y + f32(c)
    s = x + x * y * s
    s = s * jnp.where(wave == 0.0, jnp.sqrt(unit), jnp.sqrt(2.0 * unit))
    return jnp.where((wave < size) & (place < size) & (place >= 0.0), s, 0.0)


def cells_kernel(
    planes,
    mine_ref,
    box_ref,
    x_hbm,
    even_ref,
    odd_ref,
    rim_ref,
    x_ref,
    stage0_ref,
    stage1_ref,
    table_ref,
    c_hi_ref,
    c_lo_ref,
    l_hi_ref,
    l_lo_ref,
    even_hi_ref,
    even_lo_ref,
    odd_hi_ref,
    odd_lo_ref,
    sem,
):
    mine = mine_ref[0]
    holders = box_ref.shape[1]
    fetch = pltpu.make_async_copy(x_hbm, x_ref, sem)
    fetch.start()
    low32 = iota((32, LANES), 1) < B
    low8 = iota((8, LANES), 1) < B
    lane = iota((B, LANES), 1)
    low = lane < B
    row64 = iota((B, LANES), 0).astype(f32)
    x_wave = 2 * (lane % 32) + (lane // 32) % 2
    x_wave64 = x_wave.astype(f32)
    x_wave8 = x_wave[:8].astype(f32)
    l_low = iota((144, LANES), 1) < B

    def tables(p, carry):
        ex = box_ref[0, p]
        ey = box_ref[1, p]
        c = cosine_tile(ey, row64, jnp.where(low, lane, rim_cell(lane - B, ey)).astype(f32))
        turned = pltpu.roll(c, B, 1)
        c = jnp.concatenate(
            [
                jnp.concatenate([jnp.where(low, c, 0.0), jnp.where(low, turned, 0.0)], 1),
                jnp.concatenate([jnp.where(low, 0.0, turned), jnp.where(low, 0.0, c)], 1),
            ],
            0,
        )
        c_hi_ref[p], c_lo_ref[p] = split(c)
        spot = pl.multiple_of(p * B, B)
        g = cosine_tile(ex, x_wave64, row64)
        table_ref[pl.ds(spot, B), :] = g
        edge = cosine_tile(ex, x_wave8, rim_cell(iota((8, LANES), 0), ex).astype(f32))
        rows = jnp.concatenate(
            [
                table_ref[pl.ds(spot, 32, stride=2), :],
                pltpu.roll(table_ref[pl.ds(spot + 1, 32, stride=2), :], 32, 1),
                edge,
                jnp.zeros((8, LANES), f32),
                g,
            ],
            0,
        )
        l_hi, l_lo = split(rows)
        l_hi_ref[p] = l_hi
        l_lo_ref[p] = jnp.where(l_low, l_lo, jnp.zeros_like(l_lo))
        return carry

    lax.fori_loop(0, holders, tables, 0)
    fetch.wait()

    def along_y(p, r_hi_ref, r_lo_ref):
        x = jnp.concatenate(
            [x_ref[pl.ds(kz * 256 + p, 32, stride=8), :] for kz in range(planes)], 0
        )
        c_hi, c_lo = c_hi_ref[p], c_lo_ref[p]
        x_hi, x_lo = split(x)
        t = dot(
            jnp.concatenate([x_hi, x_hi, x_lo], 1), jnp.concatenate([c_hi, c_lo, c_hi], 0)
        )
        main = [t[kz * 32 : (kz + 1) * 32, :LANES] for kz in range(planes)]
        rims = t[0:32, LANES:]
        for kz in range(1, planes):
            rims = rims + pltpu.roll(t[kz * 32 : (kz + 1) * 32, LANES:], kz * RIM, 1)
        main.append(rims)
        for i, part in enumerate(main):
            hi, lo = split(jnp.concatenate([part, pltpu.roll(part, B, 1)], 0))
            r_hi_ref[:, i * LANES : (i + 1) * LANES] = hi
            r_lo_ref[:, i * LANES : (i + 1) * LANES] = lo

    def along_x(p, r_hi_ref, r_lo_ref, stage_ref):
        r_hi, r_lo = r_hi_ref[...], r_lo_ref[...]
        right = jnp.concatenate([r_hi, r_lo, r_hi, r_lo], 0)
        left = jnp.concatenate([l_hi_ref[p], l_lo_ref[p]], 1)
        y = dot(left[:80], right[:, : planes * LANES])
        z = dot(left[80:], right[:, planes * LANES :])
        for kz in range(planes):
            tile = y[:, kz * LANES : (kz + 1) * LANES]
            out = jnp.where(low32, tile[:32], tile[32:64])
            stage_ref[kz * 32 : (kz + 1) * 32, :] = out
            for s in range(8):
                spot = (s // 2) * 256 + kz * 32 + p
                (even_ref, odd_ref)[s % 2][pl.ds(spot, 4, stride=8), :] = stage_ref[
                    pl.ds(kz * 32 + (mine ^ s) * 4, 4), :
                ]
            rim_ref[pl.ds(pl.multiple_of(p * 128 + kz * RIM, RIM), RIM), :] = jnp.where(
                low8, tile[64:72], 0.0
            )
        rim_ref[pl.ds(pl.multiple_of(p * 128 + 64, 64), 64), :] = jnp.concatenate(
            [z.T[:64], jnp.zeros((64, 64), f32)], 1
        )

    even = (even_hi_ref, even_lo_ref)
    odd = (odd_hi_ref, odd_lo_ref)

    def two(i, carry):
        along_y(2 * i + 1, *odd)
        along_x(2 * i, *even, stage0_ref)
        along_y(jnp.minimum(2 * i + 2, holders - 1), *even)
        along_x(2 * i + 1, *odd, stage1_ref)
        return carry

    along_y(0, *even)
    lax.fori_loop(0, holders // 2, two, 0)


def pack_kernel(planes, face_hbm, rim_ref, pay_hbm, rim_hbm, face_ref, used_ref, pay_ref, sems):
    fetch = pltpu.make_async_copy(face_hbm, face_ref, sems.at[2])
    fetch.start()
    keep = pltpu.make_async_copy(rim_ref, rim_hbm, sems.at[0])
    keep.start()
    pay_ref[...] = jnp.zeros_like(pay_ref)
    targets = pay_ref.shape[0] // FACE_ROWS

    def clear(t, carry):
        used_ref[t] = 0
        return carry

    lax.fori_loop(0, targets, clear, 0, unroll=8)
    fetch.wait()

    lane = iota((planes, LANES), 1)

    def face(r, carry):
        length = face_ref[3, r]
        live = (length > 0).astype(jnp.int32)
        side = face_ref[1, r]
        target = face_ref[4, r] * live
        code = face_ref[5, r] * 4 + face_ref[6, r] + 1
        slot = used_ref[target] * live
        used_ref[target] = used_ref[target] + live
        first = slot * B + face_ref[7, r]
        turn = (first - face_ref[2, r] + LANES) & (LANES - 1)
        base = face_ref[0, r] * 128 + (side >> 1) * 64 + (side & 1) * 3
        here = (lane >= first) & (lane < first + length)
        for j in range(3):
            values = pltpu.roll(rim_ref[pl.ds(base + j, planes, stride=RIM), :], turn, 1)
            rows = pl.ds(target * FACE_ROWS + j * planes, planes)
            pltpu.store(pay_ref.at[rows, :], values, mask=here)
        rows = pl.ds(target * FACE_ROWS + 3 * planes, 1)
        label = jnp.full((1, LANES), code, jnp.int32).astype(f32)
        pltpu.store(pay_ref.at[rows, :], label, mask=here[:1])
        return carry

    lax.fori_loop(0, face_ref.shape[1], face, 0, unroll=4)
    send = pltpu.make_async_copy(pay_ref, pay_hbm, sems.at[1])
    send.start()
    keep.wait()
    send.wait()


def depth_kernel(planes, table_ref, own_ref, near_ref, *refs):
    far, outs = refs[:-2], refs[-2:]
    count = 2 + 2 * len(far)
    size = 32 * planes
    blocks = [(own_ref, 0), (near_ref, 0)] + [(r, i * size) for r in far for i in range(2)]
    total = count * planes
    t_hi, t_lo = split(table_ref[...])
    t_lo = jnp.where(iota((total, LANES), 1) < total, t_lo, jnp.zeros_like(t_lo))
    left = jnp.concatenate([t_hi, t_lo], 1)
    for q in range(4):
        right = jnp.concatenate(
            [
                jnp.concatenate(
                    [b[pl.ds(at + q * 8 + p, planes, stride=32), :] for b, at in blocks], 0
                )
                for p in range(8)
            ],
            1,
        )
        r_hi, r_lo = split(right)
        mixed = dot(left, jnp.concatenate([r_hi, r_lo, r_hi, r_lo], 0))
        for p in range(8):
            for s in range(count):
                spot = (s // 2) * size + q * 8 + p
                outs[s % 2][pl.ds(spot, planes, stride=32), :] = mixed[
                    s * planes : (s + 1) * planes, p * LANES : (p + 1) * LANES
                ]


def advance_kernel(
    planes,
    total,
    mine_ref,
    box_ref,
    got_ref,
    rim_hbm,
    now_hbm,
    prev_hbm,
    col_hbm,
    row_hbm,
    edge_row_hbm,
    edge_col_hbm,
    out_ref,
    sum_ref,
    times_ref,
    now_ref,
    prev_ref,
    rim_ref,
    col_ref,
    row_ref,
    edge_row_ref,
    edge_col_ref,
    label_ref,
    code_ref,
    even_down_ref,
    even_hi_ref,
    even_lo_ref,
    odd_down_ref,
    odd_hi_ref,
    odd_lo_ref,
    sems,
):
    holders = col_hbm.shape[0]
    fetches = [
        pltpu.make_async_copy(rim_hbm, rim_ref, sems.at[0]),
        pltpu.make_async_copy(col_hbm, col_ref, sems.at[1]),
        pltpu.make_async_copy(row_hbm, row_ref, sems.at[2]),
        pltpu.make_async_copy(edge_row_hbm, edge_row_ref, sems.at[3]),
        pltpu.make_async_copy(edge_col_hbm, edge_col_ref, sems.at[4]),
        pltpu.make_async_copy(now_hbm, now_ref, sems.at[5]),
        pltpu.make_async_copy(prev_hbm, prev_ref, sems.at[6]),
    ]
    sources = got_ref.shape[0] // FACE_ROWS
    labels = got_ref[pl.ds(3 * planes, sources, stride=FACE_ROWS), :]
    place = iota((sources, LANES), 1)
    first = jnp.max(jnp.where(place < B, labels, 0.0), 1, keepdims=True)
    second = jnp.max(jnp.where(place < B, 0.0, labels), 1, keepdims=True)
    label_ref[...] = jnp.where(place == 0, first, second).astype(jnp.int32)
    to_scalars = pltpu.make_async_copy(label_ref, code_ref, sems.at[7])
    to_scalars.start()
    for copy in fetches:
        copy.start()
    sum_ref[...] = jnp.zeros_like(sum_ref)
    times_ref[...] = jnp.zeros_like(times_ref)

    to_scalars.wait()

    low = iota((RIM, LANES), 1) < B
    row = iota((RIM, LANES), 0)

    def gather(source, carry):
        codes = (code_ref[source, 0], code_ref[source, 1])

        @pl.when(codes[0] + codes[1] > 0)
        def _():
            base = source * FACE_ROWS
            marks = jnp.broadcast_to(got_ref[pl.ds(base + 3 * planes, 1), :], (RIM, LANES))
            layers = [got_ref[pl.ds(base + j * planes, planes), :] for j in range(3)]
            for slot in range(2):
                code = codes[slot]
                if slot == 1:
                    marks = pltpu.roll(marks, B, 1)
                    layers = [pltpu.roll(x, B, 1) for x in layers]
                here = (marks == code.astype(f32)) & (marks > 0.0) & low
                which = jnp.maximum(code - 1, 0)
                tile = which >> 1
                first = (which & 1) * 3
                for j in range(3):
                    rows = pl.ds(pl.multiple_of(tile * 64 + (first + j) * planes, 8), planes)
                    sum_ref[rows, :] = sum_ref[rows, :] + jnp.where(here, layers[j], 0.0)
                hit = here & (row >= first) & (row < first + 3)
                rows = pl.ds(pl.multiple_of(tile * RIM, RIM), RIM)
                times_ref[rows, :] = times_ref[rows, :] + jnp.where(hit, 1.0, 0.0)

        return carry

    lax.fori_loop(0, sources, gather, 0)
    first_plane = mine_ref[0] * planes
    lane = iota((32, LANES), 1)
    half = iota((RIM, LANES), 1) < B

    def faces(p, down_ref, right_hi_ref, right_lo_ref):
        jumps = []
        for axis in range(2):
            rows = pl.ds(pl.multiple_of((p * 2 + axis) * 64, 64), 64)
            times = times_ref[pl.ds(pl.multiple_of((p * 2 + axis) * RIM, RIM), RIM), :]
            times = jnp.concatenate([times] * planes, 0)
            came = jnp.concatenate(
                [
                    sum_ref[pl.ds((p * 2 + axis) * 64 + kz, RIM, stride=planes), :]
                    for kz in range(planes)
                ],
                0,
            )
            jumps.append(split(came - times * rim_ref[rows, :]))
        j_hi, j_lo = jumps[0]
        c_hi, c_lo = split(jnp.concatenate([col_ref[p], jnp.zeros((B, LANES), f32)], 0))
        along_y = dot(
            jnp.concatenate([j_hi, j_hi, j_lo], 1), jnp.concatenate([c_hi, c_lo, c_hi], 0)
        )
        j_hi, j_lo = jumps[1]
        r_hi, r_lo = split(row_ref[p])
        along_x = lax.dot_general(
            jnp.concatenate([r_hi, r_lo, r_hi], 1),
            jnp.concatenate([j_hi, j_hi, j_lo], 1),
            (((1,), (1,)), ((), ())),
            preferred_element_type=f32,
        )
        down_ref[...] = jnp.concatenate([along_x[:32], along_x[32:]], 1)
        for kz in range(planes):
            tile = along_y[kz * RIM : (kz + 1) * RIM]
            both = jnp.concatenate([jnp.where(half, tile, 0.0), jnp.where(half, 0.0, tile)], 0)
            hi, lo = split(both)
            right_hi_ref[:, kz * LANES : (kz + 1) * LANES] = hi
            right_lo_ref[:, kz * LANES : (kz + 1) * LANES] = lo

    def finish(p, down_ref, right_hi_ref, right_lo_ref):
        edge = edge_row_ref[p]
        edge_hi = edge.astype(bf16).astype(f32)
        edge = jnp.where(lane < 4 * RIM, edge_hi, edge - edge_hi).astype(bf16)
        right_hi = right_hi_ref[...]
        across_x = dot(
            edge[:, : 6 * RIM], jnp.concatenate([right_hi, right_lo_ref[...], right_hi], 0)
        )
        down = down_ref[...]
        down_hi = down.astype(bf16).astype(f32)
        down_lo = down - down_hi
        left_hi = []
        left_lo = []
        for kz in range(planes):
            mine = (lane // RIM) % planes == kz
            left_hi.append(jnp.where(mine, down_hi, 0.0).astype(bf16))
            left_lo.append(jnp.where(mine, down_lo, 0.0).astype(bf16))
        left_hi = jnp.concatenate(left_hi, 0)
        left_lo = jnp.concatenate(left_lo, 0)
        edges = edge_col_ref[p]
        edges = jnp.concatenate([edges[:RIM]] * planes + [edges[RIM:]] * planes, 0)
        edges_hi, edges_lo = split(edges)
        across_y = dot(
            jnp.concatenate([left_hi, left_hi, left_lo], 1),
            jnp.concatenate([edges_hi, edges_lo, edges_hi], 0),
        )
        ex = box_ref[0, p]
        ey = box_ref[1, p]
        wave_x = 2 * iota((32, LANES), 0) + lane // B
        wave_y = lane % B
        inside = (wave_x < ex) & (wave_y < ey)
        unit = TIME_STEP * np.pi
        scale_x = unit / jnp.full((1, LANES), ex, jnp.int32).astype(f32)
        scale_y = unit / jnp.full((1, LANES), ey, jnp.int32).astype(f32)
        flat = (wave_x.astype(f32) * scale_x) ** 2 + (wave_y.astype(f32) * scale_y) ** 2
        for kz in range(planes):
            depth = (first_plane + kz).astype(f32) * (unit / total)
            u = flat + depth * depth
            s = f32(WAVE[-1])
            for c in WAVE[-2::-1]:
                s = s * u + f32(c)
            rows = pl.ds(kz * 256 + p, 32, stride=8)
            new = (2.0 - u * s) * now_ref[rows, :] - prev_ref[rows, :]
            force = across_x[:, kz * LANES : (kz + 1) * LANES] + across_y[kz * 32 : (kz + 1) * 32]
            new = new + s * (force * (TIME_STEP * TIME_STEP))
            out_ref[rows, :] = jnp.where(inside, new, 0.0)

    def two(i, carry):
        faces(2 * i + 1, *odd)
        finish(2 * i, *even)
        faces(jnp.minimum(2 * i + 2, holders - 1), *even)
        finish(2 * i + 1, *odd)
        return carry

    even = (even_down_ref, even_hi_ref, even_lo_ref)
    odd = (odd_down_ref, odd_hi_ref, odd_lo_ref)
    for copy in fetches[:5]:
        copy.wait()
    faces(0, *even)
    for copy in fetches[5:]:
        copy.wait()
    lax.fori_loop(0, holders // 2, two, 0)


def tables_kernel(box_ref, *refs):
    outs, held, sems = refs[:4], refs[4:8], refs[8]
    col_ref, row_ref, edge_row_ref, edge_col_ref = held
    down = iota((B, LANES), 0)
    lane = iota((B, LANES), 1)
    col_wave = (lane % B).astype(f32)
    row_wave = (2 * (down % 32) + down // 32).astype(f32)
    across = lane.astype(f32)
    below = down.astype(f32)
    low = lane < B

    def weights(index):
        layer = index % 3
        table = [jnp.zeros(index.shape, f32)] * 3
        for i in range(3):
            for j in range(3 - i):
                table[i] = jnp.where((layer == j) & (index < 6), STENCIL[i + j], table[i])
        return table

    row_lane = lane[:32]
    row_index = row_lane % 8
    row_weights = weights(row_index)
    edge_row_wave = (2 * down[:32] + (row_lane // 8) % 2).astype(f32)
    col_index = down[:16] % 8
    col_mine = down[:16] // 8 == lane[:16] // B
    col_weights = [jnp.where(col_mine, w, 0.0) for w in weights(col_index)]
    edge_col_wave = col_wave[:16]

    def one(p, carry):
        ex = box_ref[0, p]
        ey = box_ref[1, p]
        col_ref[p] = cosine_tile(ey, col_wave, below)
        row_ref[p] = jnp.where(low, cosine_tile(ex, row_wave, across), 0.0)
        for extent, wave, index, weight, ref in (
            (ex, edge_row_wave, row_index, row_weights, edge_row_ref),
            (ey, edge_col_wave, col_index, col_weights, edge_col_ref),
        ):
            total = jnp.zeros(wave.shape, f32)
            for i in range(3):
                cell = jnp.where(index < 3, i, extent - 1 - i).astype(f32)
                total = total + weight[i] * cosine_tile(extent, wave, cell)
            ref[p] = total
        return carry

    lax.fori_loop(0, box_ref.shape[1], one, 0, unroll=2)
    copies = [pltpu.make_async_copy(h, o, sems.at[i]) for i, (h, o) in enumerate(zip(held, outs))]
    for copy in copies:
        copy.start()
    for copy in copies:
        copy.wait()


def join_kernel(planes, mine_ref, own_ref, near_ref, *refs):
    far, out_ref, sems = refs[:-2], refs[-2], refs[-1]
    mine = mine_ref[0]
    blocks = [own_ref.at[:planes], near_ref.at[:planes]]
    blocks += [r.at[pl.ds(i * planes, planes)] for r in far for i in range(2)]
    copies = []
    for s, block in enumerate(blocks):
        spot = pl.multiple_of((mine ^ s) * 32, 32)
        copies.append(pltpu.make_async_copy(block, out_ref.at[:, pl.ds(spot, 32), :], sems.at[s]))
    for copy in copies:
        copy.start()
    for copy in copies:
        copy.wait()


HB = pl.BlockSpec(memory_space=pltpu.HBM)
VM = pl.BlockSpec(memory_space=pltpu.VMEM)
SM = pl.BlockSpec(memory_space=pltpu.SMEM)


def call(kernel, args, spots, outs, scratch=(), spot=VM):
    return pl.pallas_call(
        kernel,
        out_shape=outs,
        in_specs=spots,
        out_specs=tuple(spot) if isinstance(spot, list) else jax.tree.map(lambda _: spot, outs),
        scratch_shapes=list(scratch),
        compiler_params=pltpu.CompilerParams(vmem_limit_bytes=16 * 2**20),
        cost_estimate=pl.CostEstimate(flops=10**8, bytes_accessed=4 * 2**20, transcendentals=0),
    )(*args)


def swap(block, step):
    count = lax.axis_size("height")
    return lax.ppermute(block, "height", [(i, i ^ step) for i in range(count)])


def across(blocks, near):
    size = blocks.shape[0] // 4
    return [
        swap(
            jnp.concatenate(
                [blocks[t * size : (t + 1) * size], near[t * size : (t + 1) * size]], 0
            ),
            2 * t,
        )
        for t in range(1, 4)
    ]


def in_hbm(x):
    return pltpu.with_memory_space_constraint(x, pltpu.HBM)


def tiles(field):
    planes, holders, cells = field.shape
    split_up = field.reshape(planes, holders, cells // LANES, LANES).transpose(0, 2, 1, 3)
    return split_up.reshape(-1, LANES)


def untiles(rows, planes, holders):
    cells = rows.shape[0] // (planes * holders)
    folded = rows.reshape(planes, cells, holders, LANES).transpose(0, 2, 1, 3)
    return folded.reshape(planes, holders, cells * LANES)


def step(modes_now, modes_prev, partition_boxes, face_table):
    planes, holders, _ = modes_now.shape
    count = lax.axis_size("height")
    domains = lax.axis_size("dom")
    total = planes * count
    mine = lax.axis_index("height").astype(jnp.int32)
    now = in_hbm(tiles(modes_now))
    prev = in_hbm(tiles(modes_prev))
    mine_word = mine.reshape(1)
    boxes = in_hbm(partition_boxes.T)
    face_rows = in_hbm(face_table.T)

    def rows(n):
        return jax.ShapeDtypeStruct((n, LANES), f32)

    half = 1024
    even, odd, rim = call(
        functools.partial(cells_kernel, planes),
        (mine_word, boxes, now),
        [SM, SM, HB],
        (rows(half), rows(half), rows(holders * 128)),
        [
            pltpu.VMEM((2048, LANES), f32),
            pltpu.VMEM((32 * planes, LANES), f32),
            pltpu.VMEM((32 * planes, LANES), f32),
            pltpu.VMEM((holders * B, LANES), f32),
            pltpu.VMEM((holders, LANES, 2 * LANES), bf16),
            pltpu.VMEM((holders, LANES, 2 * LANES), bf16),
            pltpu.VMEM((holders, 144, LANES), bf16),
            pltpu.VMEM((holders, 144, LANES), bf16),
            pltpu.VMEM((B, (planes + 1) * LANES), bf16),
            pltpu.VMEM((B, (planes + 1) * LANES), bf16),
            pltpu.VMEM((B, (planes + 1) * LANES), bf16),
            pltpu.VMEM((B, (planes + 1) * LANES), bf16),
            pltpu.SemaphoreType.DMA,
        ],
    )
    pay, rim = call(
        functools.partial(pack_kernel, planes),
        (face_rows, rim),
        [HB, VM],
        (rows(domains * FACE_ROWS), pltpu.HBM((holders * 128, LANES), f32)),
        [
            pltpu.SMEM(face_rows.shape, jnp.int32),
            pltpu.SMEM((domains,), jnp.int32),
            pltpu.VMEM((domains * FACE_ROWS, LANES), f32),
            pltpu.SemaphoreType.DMA((3,)),
        ],
        spot=HB,
    )
    near = swap(odd, 1)
    far = across(even, near)
    arrived = lax.all_to_all(pay.reshape(-1, 1, LANES), "dom", 0, 0, tiled=True)

    order = (mine ^ jnp.arange(count, dtype=jnp.int32))[:, None] * planes
    order = (order + jnp.arange(planes, dtype=jnp.int32)).reshape(-1)
    depth_table = cosine(jnp.full((), total, jnp.int32), order[None, :], order[:, None])
    depth_table = jnp.concatenate([depth_table, depth_table], 1)
    mixed = call(
        functools.partial(depth_kernel, planes),
        (depth_table, even, near, *far),
        [VM] * (3 + len(far)),
        (rows(half),) * 2,
    )
    back_near = swap(mixed[1], 1)
    back_far = across(mixed[0], back_near)

    later, _ = lax.optimization_barrier((boxes, mixed[0]))
    tables = call(
        tables_kernel,
        (later,),
        [SM],
        tuple(
            pltpu.HBM((holders, n, LANES), f32) for n in (B, B, 32, 2 * RIM)
        ),
        [
            pltpu.VMEM((holders, B, LANES), f32),
            pltpu.VMEM((holders, B, LANES), f32),
            pltpu.VMEM((holders, 32, LANES), f32),
            pltpu.VMEM((holders, 2 * RIM, LANES), f32),
            pltpu.SemaphoreType.DMA((4,)),
        ],
        spot=HB,
    )
    new = call(
        functools.partial(advance_kernel, planes, total),
        (mine_word, boxes, arrived.reshape(-1, LANES), in_hbm(rim), now, prev)
        + tuple(in_hbm(t) for t in tables),
        [SM] * 2 + [VM] + [HB] * 7,
        rows(2048),
        [
            pltpu.VMEM((holders * 128, LANES), f32),
            pltpu.VMEM((holders * 2 * RIM, LANES), f32),
            pltpu.VMEM((2048, LANES), f32),
            pltpu.VMEM((2048, LANES), f32),
            pltpu.VMEM((holders * 128, LANES), f32),
            pltpu.VMEM((holders, B, LANES), f32),
            pltpu.VMEM((holders, B, LANES), f32),
            pltpu.VMEM((holders, 32, LANES), f32),
            pltpu.VMEM((holders, 16, LANES), f32),
            pltpu.VMEM((domains, LANES), jnp.int32),
            pltpu.SMEM((domains, LANES), jnp.int32),
        ]
        + [
            pltpu.VMEM((32, LANES), f32),
            pltpu.VMEM((2 * RIM, planes * LANES), bf16),
            pltpu.VMEM((2 * RIM, planes * LANES), bf16),
        ]
        * 2
        + [pltpu.SemaphoreType.DMA((8,))],
    )
    pressure = call(
        functools.partial(join_kernel, planes),
        (mine_word, *[b.reshape(-1, 32, LANES) for b in (mixed[0], back_near, *back_far)]),
        [SM] + [VM] * (2 + len(back_far)),
        jax.ShapeDtypeStruct((planes, 256, LANES), f32),
        [pltpu.SemaphoreType.DMA((count,))],
        spot=HB,
    )
    pressure = untiles(pressure.reshape(-1, LANES), planes, holders)
    return untiles(new, planes, holders), pressure


def solution(mesh):
    placed = (P("height", "dom", None), P("height", "dom", None), P("dom", None), P("dom", None))
    return jax.shard_map(
        step,
        mesh=mesh,
        in_specs=placed,
        out_specs=(P("height", "dom", None), P("height", "dom", None)),
        check_vma=False,
    )
```

```python
import functools

import jax
import jax.numpy as jnp
import numpy as np
from jax import lax
from jax.experimental import pallas as pl
from jax.experimental.pallas import tpu as pltpu
from jax.sharding import PartitionSpec as P


B = 64
LANES = 128
FACE_ROWS = 25
RIM = 8

COUPLING = 32.0
STENCIL = (COUPLING * 270.0 / 180.0, COUPLING * -27.0 / 180.0, COUPLING * 2.0 / 180.0)
TIME_STEP = 0.4
WAVE = (
    0.9999999998806415,
    -0.08333333151883045,
    0.002777773302928117,
    -4.959913250130888e-05,
    5.494915434656933e-07,
    -3.861085658928547e-09,
)


bf16 = jnp.bfloat16
f32 = jnp.float32


def cosine(length, wave, place):
    angle = wave * (2 * place + 1)
    period = 4 * length
    turns = jnp.floor((angle.astype(f32) + 0.5) / period.astype(f32)).astype(jnp.int32)
    angle = angle - turns * period
    angle = jnp.minimum(angle, period - angle)
    x = (length - angle).astype(f32) * ((np.pi / 2) / length.astype(f32))
    y = x * x
    s = f32(-2.50521084e-8)
    for c in (2.75573192e-6, -1.98412698e-4, 8.33333333e-3, -1.66666667e-1):
        s = s * y + f32(c)
    s = x + x * y * s
    scale = jnp.sqrt(jnp.where(wave == 0, 1.0, 2.0) / length.astype(f32))
    inside = (wave < length) & (place < length) & (place >= 0)
    return jnp.where(inside, scale * s, 0.0)


def iota(shape, axis):
    return lax.broadcasted_iota(jnp.int32, shape, axis)


def rim_cell(index, extent):
    return jnp.where(index < 3, index, jnp.where(index < 6, extent + 2 - index, -1))


def split(x):
    hi = x.astype(bf16)
    lo = (x - hi.astype(f32)).astype(bf16)
    return hi, lo


def dot(a, b):
    return jnp.dot(a, b, preferred_element_type=f32)


def cosine_tile(length, wave, place):
    size = jnp.full((1, LANES), length, jnp.int32).astype(f32)
    unit = 1.0 / size
    angle = wave * (2.0 * place + 1.0)
    angle = angle - jnp.floor((angle + 0.5) * (0.25 * unit)) * (4.0 * size)
    angle = jnp.minimum(angle, 4.0 * size - angle)
    x = (size - angle) * (f32(np.pi / 2) * unit)
    y = x * x
    s = f32(-2.50521084e-8)
    for c in (2.75573192e-6, -1.98412698e-4, 8.33333333e-3, -1.66666667e-1):
        s = s * y + f32(c)
    s = x + x * y * s
    s = s * jnp.where(wave == 0.0, jnp.sqrt(unit), jnp.sqrt(2.0 * unit))
    return jnp.where((wave < size) & (place < size) & (place >= 0.0), s, 0.0)


def cells_kernel(
    planes,
    mine_ref,
    box_ref,
    x_hbm,
    piece0_ref,
    piece1_ref,
    piece2_ref,
    piece3_ref,
    rim_ref,
    x_ref,
    stage0_ref,
    stage1_ref,
    table_ref,
    c_hi_ref,
    c_lo_ref,
    l_hi_ref,
    l_lo_ref,
    even_hi_ref,
    even_lo_ref,
    odd_hi_ref,
    odd_lo_ref,
    sem,
):
    mine = mine_ref[0]
    piece_refs = (piece0_ref, piece1_ref, piece2_ref, piece3_ref)
    holders = box_ref.shape[1]
    fetch = pltpu.make_async_copy(x_hbm, x_ref, sem)
    fetch.start()
    low32 = iota((32, LANES), 1) < B
    low8 = iota((8, LANES), 1) < B
    lane = iota((B, LANES), 1)
    low = lane < B
    row64 = iota((B, LANES), 0).astype(f32)
    x_wave = 2 * (lane % 32) + (lane // 32) % 2
    x_wave64 = x_wave.astype(f32)
    x_wave8 = x_wave[:8].astype(f32)
    l_low = iota((144, LANES), 1) < B

    def tables(p, carry):
        ex = box_ref[0, p]
        ey = box_ref[1, p]
        c = cosine_tile(ey, row64, jnp.where(low, lane, rim_cell(lane - B, ey)).astype(f32))
        turned = pltpu.roll(c, B, 1)
        c = jnp.concatenate(
            [
                jnp.concatenate([jnp.where(low, c, 0.0), jnp.where(low, turned, 0.0)], 1),
                jnp.concatenate([jnp.where(low, 0.0, turned), jnp.where(low, 0.0, c)], 1),
            ],
            0,
        )
        c_hi_ref[p], c_lo_ref[p] = split(c)
        spot = pl.multiple_of(p * B, B)
        g = cosine_tile(ex, x_wave64, row64)
        table_ref[pl.ds(spot, B), :] = g
        edge = cosine_tile(ex, x_wave8, rim_cell(iota((8, LANES), 0), ex).astype(f32))
        rows = jnp.concatenate(
            [
                table_ref[pl.ds(spot, 32, stride=2), :],
                pltpu.roll(table_ref[pl.ds(spot + 1, 32, stride=2), :], 32, 1),
                edge,
                jnp.zeros((8, LANES), f32),
                g,
            ],
            0,
        )
        l_hi, l_lo = split(rows)
        l_hi_ref[p] = l_hi
        l_lo_ref[p] = jnp.where(l_low, l_lo, jnp.zeros_like(l_lo))
        return carry

    lax.fori_loop(0, holders, tables, 0)
    fetch.wait()

    def along_y(p, r_hi_ref, r_lo_ref):
        x = jnp.concatenate(
            [x_ref[pl.ds(kz * 256 + p, 32, stride=8), :] for kz in range(planes)], 0
        )
        c_hi, c_lo = c_hi_ref[p], c_lo_ref[p]
        x_hi, x_lo = split(x)
        t = dot(
            jnp.concatenate([x_hi, x_hi, x_lo], 1), jnp.concatenate([c_hi, c_lo, c_hi], 0)
        )
        main = [t[kz * 32 : (kz + 1) * 32, :LANES] for kz in range(planes)]
        rims = t[0:32, LANES:]
        for kz in range(1, planes):
            rims = rims + pltpu.roll(t[kz * 32 : (kz + 1) * 32, LANES:], kz * RIM, 1)
        main.append(rims)
        for i, part in enumerate(main):
            hi, lo = split(jnp.concatenate([part, pltpu.roll(part, B, 1)], 0))
            r_hi_ref[:, i * LANES : (i + 1) * LANES] = hi
            r_lo_ref[:, i * LANES : (i + 1) * LANES] = lo

    def along_x(p, r_hi_ref, r_lo_ref, stage_ref):
        r_hi, r_lo = r_hi_ref[...], r_lo_ref[...]
        right = jnp.concatenate([r_hi, r_lo, r_hi, r_lo], 0)
        left = jnp.concatenate([l_hi_ref[p], l_lo_ref[p]], 1)
        y = dot(left[:80], right[:, : planes * LANES])
        z = dot(left[80:], right[:, planes * LANES :])
        for kz in range(planes):
            tile = y[:, kz * LANES : (kz + 1) * LANES]
            out = jnp.where(low32, tile[:32], tile[32:64])
            stage_ref[kz * 32 : (kz + 1) * 32, :] = out
            for s in range(8):
                spot = (s % 2) * 256 + kz * 32 + p
                piece_refs[s // 2][pl.ds(spot, 4, stride=8), :] = stage_ref[
                    pl.ds(kz * 32 + (mine ^ s) * 4, 4), :
                ]
            rim_ref[pl.ds(pl.multiple_of(p * 128 + kz * RIM, RIM), RIM), :] = jnp.where(
                low8, tile[64:72], 0.0
            )
        rim_ref[pl.ds(pl.multiple_of(p * 128 + 64, 64), 64), :] = jnp.concatenate(
            [z.T[:64], jnp.zeros((64, 64), f32)], 1
        )

    even = (even_hi_ref, even_lo_ref)
    odd = (odd_hi_ref, odd_lo_ref)

    def two(i, carry):
        along_y(2 * i + 1, *odd)
        along_x(2 * i, *even, stage0_ref)
        along_y(jnp.minimum(2 * i + 2, holders - 1), *even)
        along_x(2 * i + 1, *odd, stage1_ref)
        return carry

    along_y(0, *even)
    lax.fori_loop(0, holders // 2, two, 0)


def pack_kernel(planes, face_hbm, rim_ref, pay_hbm, rim_hbm, face_ref, used_ref, pay_ref, sems):
    fetch = pltpu.make_async_copy(face_hbm, face_ref, sems.at[2])
    fetch.start()
    keep = pltpu.make_async_copy(rim_ref, rim_hbm, sems.at[0])
    keep.start()
    pay_ref[...] = jnp.zeros_like(pay_ref)
    targets = pay_ref.shape[0] // FACE_ROWS

    def clear(t, carry):
        used_ref[t] = 0
        return carry

    lax.fori_loop(0, targets, clear, 0, unroll=8)
    fetch.wait()

    lane = iota((planes, LANES), 1)

    def face(r, carry):
        length = face_ref[3, r]
        live = (length > 0).astype(jnp.int32)
        side = face_ref[1, r]
        target = face_ref[4, r] * live
        code = face_ref[5, r] * 4 + face_ref[6, r] + 1
        slot = used_ref[target] * live
        used_ref[target] = used_ref[target] + live
        first = slot * B + face_ref[7, r]
        turn = (first - face_ref[2, r] + LANES) & (LANES - 1)
        base = face_ref[0, r] * 128 + (side >> 1) * 64 + (side & 1) * 3
        here = (lane >= first) & (lane < first + length)
        for j in range(3):
            values = pltpu.roll(rim_ref[pl.ds(base + j, planes, stride=RIM), :], turn, 1)
            rows = pl.ds(target * FACE_ROWS + j * planes, planes)
            pltpu.store(pay_ref.at[rows, :], values, mask=here)
        rows = pl.ds(target * FACE_ROWS + 3 * planes, 1)
        label = jnp.full((1, LANES), code, jnp.int32).astype(f32)
        pltpu.store(pay_ref.at[rows, :], label, mask=here[:1])
        return carry

    lax.fori_loop(0, face_ref.shape[1], face, 0, unroll=4)
    send = pltpu.make_async_copy(pay_ref, pay_hbm, sems.at[1])
    send.start()
    keep.wait()
    send.wait()


def depth_kernel(planes, table_ref, *refs):
    ins, outs = refs[:-2], refs[-2:]
    chips = len(ins) // 2
    count = 2 * chips
    size = 32 * planes
    blocks = [(ins[s // 2 + (s % 2) * chips], 0) for s in range(count)]
    total = count * planes
    t_hi, t_lo = split(table_ref[...])
    t_lo = jnp.where(iota((total, LANES), 1) < total, t_lo, jnp.zeros_like(t_lo))
    left = jnp.concatenate([t_hi, t_lo], 1)
    for q in range(4):
        right = jnp.concatenate(
            [
                jnp.concatenate(
                    [b[pl.ds(at + q * 8 + p, planes, stride=32), :] for b, at in blocks], 0
                )
                for p in range(8)
            ],
            1,
        )
        r_hi, r_lo = split(right)
        mixed = dot(left, jnp.concatenate([r_hi, r_lo, r_hi, r_lo], 0))
        for p in range(8):
            for s in range(count):
                spot = (s // 2) * size + q * 8 + p
                outs[s % 2][pl.ds(spot, planes, stride=32), :] = mixed[
                    s * planes : (s + 1) * planes, p * LANES : (p + 1) * LANES
                ]


def advance_kernel(
    planes,
    total,
    mine_ref,
    box_ref,
    got_ref,
    rim_hbm,
    now_hbm,
    prev_hbm,
    col_hbm,
    row_hbm,
    edge_row_hbm,
    edge_col_hbm,
    out_ref,
    sum_ref,
    times_ref,
    now_ref,
    prev_ref,
    rim_ref,
    col_ref,
    row_ref,
    edge_row_ref,
    edge_col_ref,
    label_ref,
    code_ref,
    even_down_ref,
    even_hi_ref,
    even_lo_ref,
    odd_down_ref,
    odd_hi_ref,
    odd_lo_ref,
    sems,
):
    holders = col_hbm.shape[0]
    fetches = [
        pltpu.make_async_copy(rim_hbm, rim_ref, sems.at[0]),
        pltpu.make_async_copy(col_hbm, col_ref, sems.at[1]),
        pltpu.make_async_copy(row_hbm, row_ref, sems.at[2]),
        pltpu.make_async_copy(edge_row_hbm, edge_row_ref, sems.at[3]),
        pltpu.make_async_copy(edge_col_hbm, edge_col_ref, sems.at[4]),
        pltpu.make_async_copy(now_hbm, now_ref, sems.at[5]),
        pltpu.make_async_copy(prev_hbm, prev_ref, sems.at[6]),
    ]
    sources = got_ref.shape[0] // FACE_ROWS
    labels = got_ref[pl.ds(3 * planes, sources, stride=FACE_ROWS), :]
    place = iota((sources, LANES), 1)
    first = jnp.max(jnp.where(place < B, labels, 0.0), 1, keepdims=True)
    second = jnp.max(jnp.where(place < B, 0.0, labels), 1, keepdims=True)
    label_ref[...] = jnp.where(place == 0, first, second).astype(jnp.int32)
    to_scalars = pltpu.make_async_copy(label_ref, code_ref, sems.at[7])
    to_scalars.start()
    for copy in fetches:
        copy.start()
    sum_ref[...] = jnp.zeros_like(sum_ref)
    times_ref[...] = jnp.zeros_like(times_ref)

    to_scalars.wait()

    low = iota((RIM, LANES), 1) < B
    row = iota((RIM, LANES), 0)

    def gather(source, carry):
        codes = (code_ref[source, 0], code_ref[source, 1])

        @pl.when(codes[0] + codes[1] > 0)
        def _():
            base = source * FACE_ROWS
            marks = jnp.broadcast_to(got_ref[pl.ds(base + 3 * planes, 1), :], (RIM, LANES))
            layers = [got_ref[pl.ds(base + j * planes, planes), :] for j in range(3)]
            for slot in range(2):
                code = codes[slot]
                if slot == 1:
                    marks = pltpu.roll(marks, B, 1)
                    layers = [pltpu.roll(x, B, 1) for x in layers]
                here = (marks == code.astype(f32)) & (marks > 0.0) & low
                which = jnp.maximum(code - 1, 0)
                tile = which >> 1
                first = (which & 1) * 3
                for j in range(3):
                    rows = pl.ds(pl.multiple_of(tile * 64 + (first + j) * planes, 8), planes)
                    sum_ref[rows, :] = sum_ref[rows, :] + jnp.where(here, layers[j], 0.0)
                hit = here & (row >= first) & (row < first + 3)
                rows = pl.ds(pl.multiple_of(tile * RIM, RIM), RIM)
                times_ref[rows, :] = times_ref[rows, :] + jnp.where(hit, 1.0, 0.0)

        return carry

    lax.fori_loop(0, sources, gather, 0)
    first_plane = mine_ref[0] * planes
    lane = iota((32, LANES), 1)
    half = iota((RIM, LANES), 1) < B

    def faces(p, down_ref, right_hi_ref, right_lo_ref):
        jumps = []
        for axis in range(2):
            rows = pl.ds(pl.multiple_of((p * 2 + axis) * 64, 64), 64)
            times = times_ref[pl.ds(pl.multiple_of((p * 2 + axis) * RIM, RIM), RIM), :]
            times = jnp.concatenate([times] * planes, 0)
            came = jnp.concatenate(
                [
                    sum_ref[pl.ds((p * 2 + axis) * 64 + kz, RIM, stride=planes), :]
                    for kz in range(planes)
                ],
                0,
            )
            jumps.append(split(came - times * rim_ref[rows, :]))
        j_hi, j_lo = jumps[0]
        c_hi, c_lo = split(jnp.concatenate([col_ref[p], jnp.zeros((B, LANES), f32)], 0))
        along_y = dot(
            jnp.concatenate([j_hi, j_hi, j_lo], 1), jnp.concatenate([c_hi, c_lo, c_hi], 0)
        )
        j_hi, j_lo = jumps[1]
        r_hi, r_lo = split(row_ref[p])
        along_x = lax.dot_general(
            jnp.concatenate([r_hi, r_lo, r_hi], 1),
            jnp.concatenate([j_hi, j_hi, j_lo], 1),
            (((1,), (1,)), ((), ())),
            preferred_element_type=f32,
        )
        down_ref[...] = jnp.concatenate([along_x[:32], along_x[32:]], 1)
        for kz in range(planes):
            tile = along_y[kz * RIM : (kz + 1) * RIM]
            both = jnp.concatenate([jnp.where(half, tile, 0.0), jnp.where(half, 0.0, tile)], 0)
            hi, lo = split(both)
            right_hi_ref[:, kz * LANES : (kz + 1) * LANES] = hi
            right_lo_ref[:, kz * LANES : (kz + 1) * LANES] = lo

    def finish(p, down_ref, right_hi_ref, right_lo_ref):
        edge = edge_row_ref[p]
        edge_hi = edge.astype(bf16).astype(f32)
        edge = jnp.where(lane < 4 * RIM, edge_hi, edge - edge_hi).astype(bf16)
        right_hi = right_hi_ref[...]
        across_x = dot(
            edge[:, : 6 * RIM], jnp.concatenate([right_hi, right_lo_ref[...], right_hi], 0)
        )
        down = down_ref[...]
        down_hi = down.astype(bf16).astype(f32)
        down_lo = down - down_hi
        left_hi = []
        left_lo = []
        for kz in range(planes):
            mine = (lane // RIM) % planes == kz
            left_hi.append(jnp.where(mine, down_hi, 0.0).astype(bf16))
            left_lo.append(jnp.where(mine, down_lo, 0.0).astype(bf16))
        left_hi = jnp.concatenate(left_hi, 0)
        left_lo = jnp.concatenate(left_lo, 0)
        edges = edge_col_ref[p]
        edges = jnp.concatenate([edges[:RIM]] * planes + [edges[RIM:]] * planes, 0)
        edges_hi, edges_lo = split(edges)
        across_y = dot(
            jnp.concatenate([left_hi, left_hi, left_lo], 1),
            jnp.concatenate([edges_hi, edges_lo, edges_hi], 0),
        )
        ex = box_ref[0, p]
        ey = box_ref[1, p]
        wave_x = 2 * iota((32, LANES), 0) + lane // B
        wave_y = lane % B
        inside = (wave_x < ex) & (wave_y < ey)
        unit = TIME_STEP * np.pi
        scale_x = unit / jnp.full((1, LANES), ex, jnp.int32).astype(f32)
        scale_y = unit / jnp.full((1, LANES), ey, jnp.int32).astype(f32)
        flat = (wave_x.astype(f32) * scale_x) ** 2 + (wave_y.astype(f32) * scale_y) ** 2
        for kz in range(planes):
            depth = (first_plane + kz).astype(f32) * (unit / total)
            u = flat + depth * depth
            s = f32(WAVE[-1])
            for c in WAVE[-2::-1]:
                s = s * u + f32(c)
            rows = pl.ds(kz * 256 + p, 32, stride=8)
            new = (2.0 - u * s) * now_ref[rows, :] - prev_ref[rows, :]
            force = across_x[:, kz * LANES : (kz + 1) * LANES] + across_y[kz * 32 : (kz + 1) * 32]
            new = new + s * (force * (TIME_STEP * TIME_STEP))
            out_ref[rows, :] = jnp.where(inside, new, 0.0)

    def two(i, carry):
        faces(2 * i + 1, *odd)
        finish(2 * i, *even)
        faces(jnp.minimum(2 * i + 2, holders - 1), *even)
        finish(2 * i + 1, *odd)
        return carry

    even = (even_down_ref, even_hi_ref, even_lo_ref)
    odd = (odd_down_ref, odd_hi_ref, odd_lo_ref)
    for copy in fetches[:5]:
        copy.wait()
    faces(0, *even)
    for copy in fetches[5:]:
        copy.wait()
    lax.fori_loop(0, holders // 2, two, 0)


def tables_kernel(box_ref, *refs):
    outs, held, sems = refs[:4], refs[4:8], refs[8]
    col_ref, row_ref, edge_row_ref, edge_col_ref = held
    down = iota((B, LANES), 0)
    lane = iota((B, LANES), 1)
    col_wave = (lane % B).astype(f32)
    row_wave = (2 * (down % 32) + down // 32).astype(f32)
    across = lane.astype(f32)
    below = down.astype(f32)
    low = lane < B

    def weights(index):
        layer = index % 3
        table = [jnp.zeros(index.shape, f32)] * 3
        for i in range(3):
            for j in range(3 - i):
                table[i] = jnp.where((layer == j) & (index < 6), STENCIL[i + j], table[i])
        return table

    row_lane = lane[:32]
    row_index = row_lane % 8
    row_weights = weights(row_index)
    edge_row_wave = (2 * down[:32] + (row_lane // 8) % 2).astype(f32)
    col_index = down[:16] % 8
    col_mine = down[:16] // 8 == lane[:16] // B
    col_weights = [jnp.where(col_mine, w, 0.0) for w in weights(col_index)]
    edge_col_wave = col_wave[:16]

    def one(p, carry):
        ex = box_ref[0, p]
        ey = box_ref[1, p]
        col_ref[p] = cosine_tile(ey, col_wave, below)
        row_ref[p] = jnp.where(low, cosine_tile(ex, row_wave, across), 0.0)
        for extent, wave, index, weight, ref in (
            (ex, edge_row_wave, row_index, row_weights, edge_row_ref),
            (ey, edge_col_wave, col_index, col_weights, edge_col_ref),
        ):
            total = jnp.zeros(wave.shape, f32)
            for i in range(3):
                cell = jnp.where(index < 3, i, extent - 1 - i).astype(f32)
                total = total + weight[i] * cosine_tile(extent, wave, cell)
            ref[p] = total
        return carry

    lax.fori_loop(0, box_ref.shape[1], one, 0, unroll=2)
    copies = [pltpu.make_async_copy(h, o, sems.at[i]) for i, (h, o) in enumerate(zip(held, outs))]
    for copy in copies:
        copy.start()
    for copy in copies:
        copy.wait()


def join_kernel(planes, mine_ref, own_ref, near_ref, *refs):
    far, out_ref, sems = refs[:-2], refs[-2], refs[-1]
    mine = mine_ref[0]
    blocks = [own_ref.at[:planes], near_ref.at[:planes]]
    blocks += [r.at[pl.ds(i * planes, planes)] for r in far for i in range(2)]
    copies = []
    for s, block in enumerate(blocks):
        spot = pl.multiple_of((mine ^ s) * 32, 32)
        copies.append(pltpu.make_async_copy(block, out_ref.at[:, pl.ds(spot, 32), :], sems.at[s]))
    for copy in copies:
        copy.start()
    for copy in copies:
        copy.wait()


HB = pl.BlockSpec(memory_space=pltpu.HBM)
VM = pl.BlockSpec(memory_space=pltpu.VMEM)
SM = pl.BlockSpec(memory_space=pltpu.SMEM)


def call(kernel, args, spots, outs, scratch=(), spot=VM):
    return pl.pallas_call(
        kernel,
        out_shape=outs,
        in_specs=spots,
        out_specs=tuple(spot) if isinstance(spot, list) else jax.tree.map(lambda _: spot, outs),
        scratch_shapes=list(scratch),
        compiler_params=pltpu.CompilerParams(vmem_limit_bytes=16 * 2**20),
        cost_estimate=pl.CostEstimate(flops=10**8, bytes_accessed=4 * 2**20, transcendentals=0),
    )(*args)


def swap(block, step):
    count = lax.axis_size("height")
    return lax.ppermute(block, "height", [(i, i ^ step) for i in range(count)])


def across(blocks, near):
    size = blocks.shape[0] // 4
    return [
        swap(
            jnp.concatenate(
                [blocks[t * size : (t + 1) * size], near[t * size : (t + 1) * size]], 0
            ),
            2 * t,
        )
        for t in range(1, 4)
    ]


def in_hbm(x):
    return pltpu.with_memory_space_constraint(x, pltpu.HBM)


def tiles(field):
    planes, holders, cells = field.shape
    split_up = field.reshape(planes, holders, cells // LANES, LANES).transpose(0, 2, 1, 3)
    return split_up.reshape(-1, LANES)


def untiles(rows, planes, holders):
    cells = rows.shape[0] // (planes * holders)
    folded = rows.reshape(planes, cells, holders, LANES).transpose(0, 2, 1, 3)
    return folded.reshape(planes, holders, cells * LANES)


def step(modes_now, modes_prev, partition_boxes, face_table):
    planes, holders, _ = modes_now.shape
    count = lax.axis_size("height")
    domains = lax.axis_size("dom")
    total = planes * count
    mine = lax.axis_index("height").astype(jnp.int32)
    now = in_hbm(tiles(modes_now))
    prev = in_hbm(tiles(modes_prev))
    mine_word = mine.reshape(1)
    boxes = in_hbm(partition_boxes.T)
    face_rows = in_hbm(face_table.T)

    def rows(n):
        return jax.ShapeDtypeStruct((n, LANES), f32)

    half = 1024
    *pieces, rim = call(
        functools.partial(cells_kernel, planes),
        (mine_word, boxes, now),
        [SM, SM, HB],
        (rows(half // 2),) * 4 + (rows(holders * 128),),
        [
            pltpu.VMEM((2048, LANES), f32),
            pltpu.VMEM((32 * planes, LANES), f32),
            pltpu.VMEM((32 * planes, LANES), f32),
            pltpu.VMEM((holders * B, LANES), f32),
            pltpu.VMEM((holders, LANES, 2 * LANES), bf16),
            pltpu.VMEM((holders, LANES, 2 * LANES), bf16),
            pltpu.VMEM((holders, 144, LANES), bf16),
            pltpu.VMEM((holders, 144, LANES), bf16),
            pltpu.VMEM((B, (planes + 1) * LANES), bf16),
            pltpu.VMEM((B, (planes + 1) * LANES), bf16),
            pltpu.VMEM((B, (planes + 1) * LANES), bf16),
            pltpu.VMEM((B, (planes + 1) * LANES), bf16),
            pltpu.SemaphoreType.DMA,
        ],
    )
    pay, rim = call(
        functools.partial(pack_kernel, planes),
        (face_rows, rim),
        [HB, VM],
        (rows(domains * FACE_ROWS), pltpu.HBM((holders * 128, LANES), f32)),
        [
            pltpu.SMEM(face_rows.shape, jnp.int32),
            pltpu.SMEM((domains,), jnp.int32),
            pltpu.VMEM((domains * FACE_ROWS, LANES), f32),
            pltpu.SemaphoreType.DMA((3,)),
        ],
        spot=HB,
    )
    far = [swap(pieces[t], 2 * t) for t in range(1, 4)]
    arrived = lax.all_to_all(pay.reshape(-1, 1, LANES), "dom", 0, 0, tiled=True)

    near = [swap(x[half // 4 :], 1) for x in (pieces[0], *far)]

    order = (mine ^ jnp.arange(count, dtype=jnp.int32))[:, None] * planes
    order = (order + jnp.arange(planes, dtype=jnp.int32)).reshape(-1)
    depth_table = cosine(jnp.full((), total, jnp.int32), order[None, :], order[:, None])
    depth_table = jnp.concatenate([depth_table, depth_table], 1)
    mixed = call(
        functools.partial(depth_kernel, planes),
        (depth_table, pieces[0], *far, *near),
        [VM] * (2 + len(far) + len(near)),
        (rows(half),) * 2,
    )
    back_near = swap(mixed[1], 1)
    back_far = across(mixed[0], back_near)

    later, _ = lax.optimization_barrier((boxes, mixed[0]))
    tables = call(
        tables_kernel,
        (later,),
        [SM],
        tuple(
            pltpu.HBM((holders, n, LANES), f32) for n in (B, B, 32, 2 * RIM)
        ),
        [
            pltpu.VMEM((holders, B, LANES), f32),
            pltpu.VMEM((holders, B, LANES), f32),
            pltpu.VMEM((holders, 32, LANES), f32),
            pltpu.VMEM((holders, 2 * RIM, LANES), f32),
            pltpu.SemaphoreType.DMA((4,)),
        ],
        spot=HB,
    )
    new = call(
        functools.partial(advance_kernel, planes, total),
        (mine_word, boxes, arrived.reshape(-1, LANES), in_hbm(rim), now, prev)
        + tuple(in_hbm(t) for t in tables),
        [SM] * 2 + [VM] + [HB] * 7,
        rows(2048),
        [
            pltpu.VMEM((holders * 128, LANES), f32),
            pltpu.VMEM((holders * 2 * RIM, LANES), f32),
            pltpu.VMEM((2048, LANES), f32),
            pltpu.VMEM((2048, LANES), f32),
            pltpu.VMEM((holders * 128, LANES), f32),
            pltpu.VMEM((holders, B, LANES), f32),
            pltpu.VMEM((holders, B, LANES), f32),
            pltpu.VMEM((holders, 32, LANES), f32),
            pltpu.VMEM((holders, 16, LANES), f32),
            pltpu.VMEM((domains, LANES), jnp.int32),
            pltpu.SMEM((domains, LANES), jnp.int32),
        ]
        + [
            pltpu.VMEM((32, LANES), f32),
            pltpu.VMEM((2 * RIM, planes * LANES), bf16),
            pltpu.VMEM((2 * RIM, planes * LANES), bf16),
        ]
        * 2
        + [pltpu.SemaphoreType.DMA((8,))],
    )
    pressure = call(
        functools.partial(join_kernel, planes),
        (mine_word, *[b.reshape(-1, 32, LANES) for b in (mixed[0], back_near, *back_far)]),
        [SM] + [VM] * (2 + len(back_far)),
        jax.ShapeDtypeStruct((planes, 256, LANES), f32),
        [pltpu.SemaphoreType.DMA((count,))],
        spot=HB,
    )
    pressure = untiles(pressure.reshape(-1, LANES), planes, holders)
    return untiles(new, planes, holders), pressure


def solution(mesh):
    placed = (P("height", "dom", None), P("height", "dom", None), P("dom", None), P("dom", None))
    return jax.shard_map(
        step,
        mesh=mesh,
        in_specs=placed,
        out_specs=(P("height", "dom", None), P("height", "dom", None)),
        check_vma=False,
    )
```

```python
import functools

import jax
import jax.numpy as jnp
import numpy as np
from jax import lax
from jax.experimental import pallas as pl
from jax.experimental.pallas import tpu as pltpu
from jax.sharding import PartitionSpec as P


B = 64
LANES = 128
FACE_ROWS = 25
RIM = 8

COUPLING = 32.0
STENCIL = (COUPLING * 270.0 / 180.0, COUPLING * -27.0 / 180.0, COUPLING * 2.0 / 180.0)
TIME_STEP = 0.4
WAVE = (
    0.9999999998806415,
    -0.08333333151883045,
    0.002777773302928117,
    -4.959913250130888e-05,
    5.494915434656933e-07,
    -3.861085658928547e-09,
)


bf16 = jnp.bfloat16
f32 = jnp.float32


def cosine(length, wave, place):
    angle = wave * (2 * place + 1)
    period = 4 * length
    turns = jnp.floor((angle.astype(f32) + 0.5) / period.astype(f32)).astype(jnp.int32)
    angle = angle - turns * period
    angle = jnp.minimum(angle, period - angle)
    x = (length - angle).astype(f32) * ((np.pi / 2) / length.astype(f32))
    y = x * x
    s = f32(-2.50521084e-8)
    for c in (2.75573192e-6, -1.98412698e-4, 8.33333333e-3, -1.66666667e-1):
        s = s * y + f32(c)
    s = x + x * y * s
    scale = jnp.sqrt(jnp.where(wave == 0, 1.0, 2.0) / length.astype(f32))
    inside = (wave < length) & (place < length) & (place >= 0)
    return jnp.where(inside, scale * s, 0.0)


def iota(shape, axis):
    return lax.broadcasted_iota(jnp.int32, shape, axis)


def rim_cell(index, extent):
    return jnp.where(index < 3, index, jnp.where(index < 6, extent + 2 - index, -1))


def split(x):
    hi = x.astype(bf16)
    lo = (x - hi.astype(f32)).astype(bf16)
    return hi, lo


def dot(a, b):
    return jnp.dot(a, b, preferred_element_type=f32)


def cosine_tile(length, wave, place):
    size = jnp.full((1, LANES), length, jnp.int32).astype(f32)
    unit = 1.0 / size
    angle = wave * (2.0 * place + 1.0)
    angle = angle - jnp.floor((angle + 0.5) * (0.25 * unit)) * (4.0 * size)
    angle = jnp.minimum(angle, 4.0 * size - angle)
    x = (size - angle) * (f32(np.pi / 2) * unit)
    y = x * x
    s = f32(-2.50521084e-8)
    for c in (2.75573192e-6, -1.98412698e-4, 8.33333333e-3, -1.66666667e-1):
        s = s * y + f32(c)
    s = x + x * y * s
    s = s * jnp.where(wave == 0.0, jnp.sqrt(unit), jnp.sqrt(2.0 * unit))
    return jnp.where((wave < size) & (place < size) & (place >= 0.0), s, 0.0)


def cells_kernel(
    planes,
    mine_ref,
    box_ref,
    x_hbm,
    piece0_ref,
    piece1_ref,
    piece2_ref,
    piece3_ref,
    rim_ref,
    x_ref,
    stage0_ref,
    stage1_ref,
    table_ref,
    c_hi_ref,
    c_lo_ref,
    l_hi_ref,
    l_lo_ref,
    even_hi_ref,
    even_lo_ref,
    odd_hi_ref,
    odd_lo_ref,
    sem,
):
    mine = mine_ref[0]
    piece_refs = (piece0_ref, piece1_ref, piece2_ref, piece3_ref)
    holders = box_ref.shape[1]
    fetch = pltpu.make_async_copy(x_hbm, x_ref, sem)
    fetch.start()
    low32 = iota((32, LANES), 1) < B
    low8 = iota((8, LANES), 1) < B
    lane = iota((B, LANES), 1)
    low = lane < B
    row64 = iota((B, LANES), 0).astype(f32)
    x_wave = 2 * (lane % 32) + (lane // 32) % 2
    x_wave64 = x_wave.astype(f32)
    x_wave8 = x_wave[:8].astype(f32)
    l_low = iota((144, LANES), 1) < B

    def tables(p, carry):
        ex = box_ref[0, p]
        ey = box_ref[1, p]
        c = cosine_tile(ey, row64, jnp.where(low, lane, rim_cell(lane - B, ey)).astype(f32))
        turned = pltpu.roll(c, B, 1)
        c = jnp.concatenate(
            [
                jnp.concatenate([jnp.where(low, c, 0.0), jnp.where(low, turned, 0.0)], 1),
                jnp.concatenate([jnp.where(low, 0.0, turned), jnp.where(low, 0.0, c)], 1),
            ],
            0,
        )
        c_hi_ref[p], c_lo_ref[p] = split(c)
        spot = pl.multiple_of(p * B, B)
        g = cosine_tile(ex, x_wave64, row64)
        table_ref[pl.ds(spot, B), :] = g
        edge = cosine_tile(ex, x_wave8, rim_cell(iota((8, LANES), 0), ex).astype(f32))
        rows = jnp.concatenate(
            [
                table_ref[pl.ds(spot, 32, stride=2), :],
                pltpu.roll(table_ref[pl.ds(spot + 1, 32, stride=2), :], 32, 1),
                edge,
                jnp.zeros((8, LANES), f32),
                g,
            ],
            0,
        )
        l_hi, l_lo = split(rows)
        l_hi_ref[p] = l_hi
        l_lo_ref[p] = jnp.where(l_low, l_lo, jnp.zeros_like(l_lo))
        return carry

    lax.fori_loop(0, holders, tables, 0)
    fetch.wait()

    def along_y(p, r_hi_ref, r_lo_ref):
        x = jnp.concatenate(
            [x_ref[pl.ds(kz * 256 + p, 32, stride=8), :] for kz in range(planes)], 0
        )
        c_hi, c_lo = c_hi_ref[p], c_lo_ref[p]
        x_hi, x_lo = split(x)
        t = dot(
            jnp.concatenate([x_hi, x_hi, x_lo], 1), jnp.concatenate([c_hi, c_lo, c_hi], 0)
        )
        main = [t[kz * 32 : (kz + 1) * 32, :LANES] for kz in range(planes)]
        rims = t[0:32, LANES:]
        for kz in range(1, planes):
            rims = rims + pltpu.roll(t[kz * 32 : (kz + 1) * 32, LANES:], kz * RIM, 1)
        main.append(rims)
        for i, part in enumerate(main):
            hi, lo = split(jnp.concatenate([part, pltpu.roll(part, B, 1)], 0))
            r_hi_ref[:, i * LANES : (i + 1) * LANES] = hi
            r_lo_ref[:, i * LANES : (i + 1) * LANES] = lo

    def along_x(p, r_hi_ref, r_lo_ref, stage_ref):
        r_hi, r_lo = r_hi_ref[...], r_lo_ref[...]
        right = jnp.concatenate([r_hi, r_lo, r_hi, r_lo], 0)
        left = jnp.concatenate([l_hi_ref[p], l_lo_ref[p]], 1)
        y = dot(left[:80], right[:, : planes * LANES])
        z = dot(left[80:], right[:, planes * LANES :])
        for kz in range(planes):
            tile = y[:, kz * LANES : (kz + 1) * LANES]
            out = jnp.where(low32, tile[:32], tile[32:64])
            stage_ref[kz * 32 : (kz + 1) * 32, :] = out
            for s in range(8):
                spot = (s % 2) * 256 + kz * 32 + p
                piece_refs[s // 2][pl.ds(spot, 4, stride=8), :] = stage_ref[
                    pl.ds(kz * 32 + (mine ^ s) * 4, 4), :
                ]
            rim_ref[pl.ds(pl.multiple_of(p * 128 + kz * RIM, RIM), RIM), :] = jnp.where(
                low8, tile[64:72], 0.0
            )
        rim_ref[pl.ds(pl.multiple_of(p * 128 + 64, 64), 64), :] = jnp.concatenate(
            [z.T[:64], jnp.zeros((64, 64), f32)], 1
        )

    even = (even_hi_ref, even_lo_ref)
    odd = (odd_hi_ref, odd_lo_ref)

    def two(i, carry):
        along_y(2 * i + 1, *odd)
        along_x(2 * i, *even, stage0_ref)
        along_y(jnp.minimum(2 * i + 2, holders - 1), *even)
        along_x(2 * i + 1, *odd, stage1_ref)
        return carry

    along_y(0, *even)
    lax.fori_loop(0, holders // 2, two, 0)


def pack_kernel(planes, face_hbm, rim_ref, pay_hbm, rim_hbm, face_ref, used_ref, pay_ref, sems):
    fetch = pltpu.make_async_copy(face_hbm, face_ref, sems.at[2])
    fetch.start()
    keep = pltpu.make_async_copy(rim_ref, rim_hbm, sems.at[0])
    keep.start()
    pay_ref[...] = jnp.zeros_like(pay_ref)
    targets = pay_ref.shape[0] // FACE_ROWS

    def clear(t, carry):
        used_ref[t] = 0
        return carry

    lax.fori_loop(0, targets, clear, 0, unroll=8)
    fetch.wait()

    lane = iota((planes, LANES), 1)

    def face(r, carry):
        length = face_ref[3, r]
        live = (length > 0).astype(jnp.int32)
        side = face_ref[1, r]
        target = face_ref[4, r] * live
        code = face_ref[5, r] * 4 + face_ref[6, r] + 1
        slot = used_ref[target] * live
        used_ref[target] = used_ref[target] + live
        first = slot * B + face_ref[7, r]
        turn = (first - face_ref[2, r] + LANES) & (LANES - 1)
        base = face_ref[0, r] * 128 + (side >> 1) * 64 + (side & 1) * 3
        here = (lane >= first) & (lane < first + length)
        for j in range(3):
            values = pltpu.roll(rim_ref[pl.ds(base + j, planes, stride=RIM), :], turn, 1)
            rows = pl.ds(target * FACE_ROWS + j * planes, planes)
            pltpu.store(pay_ref.at[rows, :], values, mask=here)
        rows = pl.ds(target * FACE_ROWS + 3 * planes, 1)
        label = jnp.full((1, LANES), code, jnp.int32).astype(f32)
        pltpu.store(pay_ref.at[rows, :], label, mask=here[:1])
        return carry

    lax.fori_loop(0, face_ref.shape[1], face, 0, unroll=4)
    send = pltpu.make_async_copy(pay_ref, pay_hbm, sems.at[1])
    send.start()
    keep.wait()
    send.wait()


def depth_kernel(planes, table_ref, *refs):
    ins, outs = refs[:-2], refs[-2:]
    chips = len(ins) // 2
    count = 2 * chips
    size = 32 * planes
    blocks = [(ins[s // 2 + (s % 2) * chips], 0) for s in range(count)]
    total = count * planes
    t_hi, t_lo = split(table_ref[...])
    t_lo = jnp.where(iota((total, LANES), 1) < total, t_lo, jnp.zeros_like(t_lo))
    left = jnp.concatenate([t_hi, t_lo], 1)
    for q in range(4):
        right = jnp.concatenate(
            [
                jnp.concatenate(
                    [b[pl.ds(at + q * 8 + p, planes, stride=32), :] for b, at in blocks], 0
                )
                for p in range(8)
            ],
            1,
        )
        r_hi, r_lo = split(right)
        mixed = dot(left, jnp.concatenate([r_hi, r_lo, r_hi, r_lo], 0))
        for p in range(8):
            for s in range(count):
                spot = (s // 2) * size + q * 8 + p
                outs[s % 2][pl.ds(spot, planes, stride=32), :] = mixed[
                    s * planes : (s + 1) * planes, p * LANES : (p + 1) * LANES
                ]


def advance_kernel(
    planes,
    total,
    mine_ref,
    box_ref,
    got_ref,
    rim_hbm,
    now_hbm,
    prev_hbm,
    col_hbm,
    row_hbm,
    edge_row_hbm,
    edge_col_hbm,
    out_ref,
    sum_ref,
    times_ref,
    now_ref,
    prev_ref,
    rim_ref,
    col_ref,
    row_ref,
    edge_row_ref,
    edge_col_ref,
    label_ref,
    code_ref,
    even_down_ref,
    even_hi_ref,
    even_lo_ref,
    odd_down_ref,
    odd_hi_ref,
    odd_lo_ref,
    sems,
):
    holders = col_hbm.shape[0]
    fetches = [
        pltpu.make_async_copy(rim_hbm, rim_ref, sems.at[0]),
        pltpu.make_async_copy(col_hbm, col_ref, sems.at[1]),
        pltpu.make_async_copy(row_hbm, row_ref, sems.at[2]),
        pltpu.make_async_copy(edge_row_hbm, edge_row_ref, sems.at[3]),
        pltpu.make_async_copy(edge_col_hbm, edge_col_ref, sems.at[4]),
        pltpu.make_async_copy(now_hbm, now_ref, sems.at[5]),
        pltpu.make_async_copy(prev_hbm, prev_ref, sems.at[6]),
    ]
    sources = got_ref.shape[0] // FACE_ROWS
    labels = got_ref[pl.ds(3 * planes, sources, stride=FACE_ROWS), :]
    place = iota((sources, LANES), 1)
    first = jnp.max(jnp.where(place < B, labels, 0.0), 1, keepdims=True)
    second = jnp.max(jnp.where(place < B, 0.0, labels), 1, keepdims=True)
    label_ref[...] = jnp.where(place == 0, first, second).astype(jnp.int32)
    to_scalars = pltpu.make_async_copy(label_ref, code_ref, sems.at[7])
    to_scalars.start()
    for copy in fetches:
        copy.start()
    sum_ref[...] = jnp.zeros_like(sum_ref)
    times_ref[...] = jnp.zeros_like(times_ref)

    to_scalars.wait()

    low = iota((RIM, LANES), 1) < B
    row = iota((RIM, LANES), 0)

    def gather(source, carry):
        codes = (code_ref[source, 0], code_ref[source, 1])

        @pl.when(codes[0] + codes[1] > 0)
        def _():
            base = source * FACE_ROWS
            marks = jnp.broadcast_to(got_ref[pl.ds(base + 3 * planes, 1), :], (RIM, LANES))
            layers = [got_ref[pl.ds(base + j * planes, planes), :] for j in range(3)]
            for slot in range(2):
                code = codes[slot]
                if slot == 1:
                    marks = pltpu.roll(marks, B, 1)
                    layers = [pltpu.roll(x, B, 1) for x in layers]
                here = (marks == code.astype(f32)) & (marks > 0.0) & low
                which = jnp.maximum(code - 1, 0)
                tile = which >> 1
                first = (which & 1) * 3
                for j in range(3):
                    rows = pl.ds(pl.multiple_of(tile * 64 + (first + j) * planes, 8), planes)
                    sum_ref[rows, :] = sum_ref[rows, :] + jnp.where(here, layers[j], 0.0)
                hit = here & (row >= first) & (row < first + 3)
                rows = pl.ds(pl.multiple_of(tile * RIM, RIM), RIM)
                times_ref[rows, :] = times_ref[rows, :] + jnp.where(hit, 1.0, 0.0)

        return carry

    lax.fori_loop(0, sources, gather, 0)
    first_plane = mine_ref[0] * planes
    lane = iota((32, LANES), 1)
    half = iota((RIM, LANES), 1) < B

    def faces(p, down_ref, right_hi_ref, right_lo_ref):
        jumps = []
        for axis in range(2):
            rows = pl.ds(pl.multiple_of((p * 2 + axis) * 64, 64), 64)
            times = times_ref[pl.ds(pl.multiple_of((p * 2 + axis) * RIM, RIM), RIM), :]
            times = jnp.concatenate([times] * planes, 0)
            came = jnp.concatenate(
                [
                    sum_ref[pl.ds((p * 2 + axis) * 64 + kz, RIM, stride=planes), :]
                    for kz in range(planes)
                ],
                0,
            )
            jumps.append(split(came - times * rim_ref[rows, :]))
        j_hi, j_lo = jumps[0]
        c_hi, c_lo = split(jnp.concatenate([col_ref[p], jnp.zeros((B, LANES), f32)], 0))
        along_y = dot(
            jnp.concatenate([j_hi, j_hi, j_lo], 1), jnp.concatenate([c_hi, c_lo, c_hi], 0)
        )
        j_hi, j_lo = jumps[1]
        r_hi, r_lo = split(row_ref[p])
        along_x = lax.dot_general(
            jnp.concatenate([r_hi, r_lo, r_hi], 1),
            jnp.concatenate([j_hi, j_hi, j_lo], 1),
            (((1,), (1,)), ((), ())),
            preferred_element_type=f32,
        )
        down_ref[...] = jnp.concatenate([along_x[:32], along_x[32:]], 1)
        for kz in range(planes):
            tile = along_y[kz * RIM : (kz + 1) * RIM]
            both = jnp.concatenate([jnp.where(half, tile, 0.0), jnp.where(half, 0.0, tile)], 0)
            hi, lo = split(both)
            right_hi_ref[:, kz * LANES : (kz + 1) * LANES] = hi
            right_lo_ref[:, kz * LANES : (kz + 1) * LANES] = lo

    def finish(p, down_ref, right_hi_ref, right_lo_ref):
        edge = edge_row_ref[p]
        edge_hi = edge.astype(bf16).astype(f32)
        edge = jnp.where(lane < 4 * RIM, edge_hi, edge - edge_hi).astype(bf16)
        right_hi = right_hi_ref[...]
        across_x = dot(
            edge[:, : 6 * RIM], jnp.concatenate([right_hi, right_lo_ref[...], right_hi], 0)
        )
        down = down_ref[...]
        down_hi = down.astype(bf16).astype(f32)
        down_lo = down - down_hi
        left_hi = []
        left_lo = []
        for kz in range(planes):
            mine = (lane // RIM) % planes == kz
            left_hi.append(jnp.where(mine, down_hi, 0.0).astype(bf16))
            left_lo.append(jnp.where(mine, down_lo, 0.0).astype(bf16))
        left_hi = jnp.concatenate(left_hi, 0)
        left_lo = jnp.concatenate(left_lo, 0)
        edges = edge_col_ref[p]
        edges = jnp.concatenate([edges[:RIM]] * planes + [edges[RIM:]] * planes, 0)
        edges_hi, edges_lo = split(edges)
        across_y = dot(
            jnp.concatenate([left_hi, left_hi, left_lo], 1),
            jnp.concatenate([edges_hi, edges_lo, edges_hi], 0),
        )
        ex = box_ref[0, p]
        ey = box_ref[1, p]
        wave_x = 2 * iota((32, LANES), 0) + lane // B
        wave_y = lane % B
        inside = (wave_x < ex) & (wave_y < ey)
        unit = TIME_STEP * np.pi
        scale_x = unit / jnp.full((1, LANES), ex, jnp.int32).astype(f32)
        scale_y = unit / jnp.full((1, LANES), ey, jnp.int32).astype(f32)
        flat = (wave_x.astype(f32) * scale_x) ** 2 + (wave_y.astype(f32) * scale_y) ** 2
        for kz in range(planes):
            depth = (first_plane + kz).astype(f32) * (unit / total)
            u = flat + depth * depth
            s = f32(WAVE[-1])
            for c in WAVE[-2::-1]:
                s = s * u + f32(c)
            rows = pl.ds(kz * 256 + p, 32, stride=8)
            new = (2.0 - u * s) * now_ref[rows, :] - prev_ref[rows, :]
            force = across_x[:, kz * LANES : (kz + 1) * LANES] + across_y[kz * 32 : (kz + 1) * 32]
            new = new + s * (force * (TIME_STEP * TIME_STEP))
            out_ref[rows, :] = jnp.where(inside, new, 0.0)

    def two(i, carry):
        faces(2 * i + 1, *odd)
        finish(2 * i, *even)
        faces(jnp.minimum(2 * i + 2, holders - 1), *even)
        finish(2 * i + 1, *odd)
        return carry

    even = (even_down_ref, even_hi_ref, even_lo_ref)
    odd = (odd_down_ref, odd_hi_ref, odd_lo_ref)
    for copy in fetches[:5]:
        copy.wait()
    faces(0, *even)
    for copy in fetches[5:]:
        copy.wait()
    lax.fori_loop(0, holders // 2, two, 0)


def tables_kernel(box_ref, *refs):
    outs, held, sems = refs[:4], refs[4:8], refs[8]
    col_ref, row_ref, edge_row_ref, edge_col_ref = held
    down = iota((B, LANES), 0)
    lane = iota((B, LANES), 1)
    col_wave = (lane % B).astype(f32)
    row_wave = (2 * (down % 32) + down // 32).astype(f32)
    across = lane.astype(f32)
    below = down.astype(f32)
    low = lane < B

    def weights(index):
        layer = index % 3
        table = [jnp.zeros(index.shape, f32)] * 3
        for i in range(3):
            for j in range(3 - i):
                table[i] = jnp.where((layer == j) & (index < 6), STENCIL[i + j], table[i])
        return table

    row_lane = lane[:32]
    row_index = row_lane % 8
    row_weights = weights(row_index)
    edge_row_wave = (2 * down[:32] + (row_lane // 8) % 2).astype(f32)
    col_index = down[:16] % 8
    col_mine = down[:16] // 8 == lane[:16] // B
    col_weights = [jnp.where(col_mine, w, 0.0) for w in weights(col_index)]
    edge_col_wave = col_wave[:16]

    def one(p, carry):
        ex = box_ref[0, p]
        ey = box_ref[1, p]
        col_ref[p] = cosine_tile(ey, col_wave, below)
        row_ref[p] = jnp.where(low, cosine_tile(ex, row_wave, across), 0.0)
        for extent, wave, index, weight, ref in (
            (ex, edge_row_wave, row_index, row_weights, edge_row_ref),
            (ey, edge_col_wave, col_index, col_weights, edge_col_ref),
        ):
            total = jnp.zeros(wave.shape, f32)
            for i in range(3):
                cell = jnp.where(index < 3, i, extent - 1 - i).astype(f32)
                total = total + weight[i] * cosine_tile(extent, wave, cell)
            ref[p] = total
        return carry

    lax.fori_loop(0, box_ref.shape[1], one, 0, unroll=2)
    copies = [pltpu.make_async_copy(h, o, sems.at[i]) for i, (h, o) in enumerate(zip(held, outs))]
    for copy in copies:
        copy.start()
    for copy in copies:
        copy.wait()


def join_kernel(planes, mine_ref, own_ref, near_ref, *refs):
    far, out_ref, sems = refs[:-2], refs[-2], refs[-1]
    mine = mine_ref[0]
    blocks = [own_ref.at[:planes], near_ref.at[:planes]]
    blocks += [r.at[pl.ds(i * planes, planes)] for r in far for i in range(2)]
    copies = []
    for s, block in enumerate(blocks):
        spot = pl.multiple_of((mine ^ s) * 32, 32)
        copies.append(pltpu.make_async_copy(block, out_ref.at[:, pl.ds(spot, 32), :], sems.at[s]))
    for copy in copies:
        copy.start()
    for copy in copies:
        copy.wait()


HB = pl.BlockSpec(memory_space=pltpu.HBM)
VM = pl.BlockSpec(memory_space=pltpu.VMEM)
SM = pl.BlockSpec(memory_space=pltpu.SMEM)


def call(kernel, args, spots, outs, scratch=(), spot=VM):
    return pl.pallas_call(
        kernel,
        out_shape=outs,
        in_specs=spots,
        out_specs=tuple(spot) if isinstance(spot, list) else jax.tree.map(lambda _: spot, outs),
        scratch_shapes=list(scratch),
        compiler_params=pltpu.CompilerParams(vmem_limit_bytes=16 * 2**20),
        cost_estimate=pl.CostEstimate(flops=10**8, bytes_accessed=4 * 2**20, transcendentals=0),
    )(*args)


def swap(block, step):
    count = lax.axis_size("height")
    return lax.ppermute(block, "height", [(i, i ^ step) for i in range(count)])


def in_hbm(x):
    return pltpu.with_memory_space_constraint(x, pltpu.HBM)


def tiles(field):
    planes, holders, cells = field.shape
    split_up = field.reshape(planes, holders, cells // LANES, LANES).transpose(0, 2, 1, 3)
    return split_up.reshape(-1, LANES)


def untiles(rows, planes, holders):
    cells = rows.shape[0] // (planes * holders)
    folded = rows.reshape(planes, cells, holders, LANES).transpose(0, 2, 1, 3)
    return folded.reshape(planes, holders, cells * LANES)


def step(modes_now, modes_prev, partition_boxes, face_table):
    planes, holders, _ = modes_now.shape
    count = lax.axis_size("height")
    domains = lax.axis_size("dom")
    total = planes * count
    mine = lax.axis_index("height").astype(jnp.int32)
    now = in_hbm(tiles(modes_now))
    prev = in_hbm(tiles(modes_prev))
    mine_word = mine.reshape(1)
    boxes = in_hbm(partition_boxes.T)
    face_rows = in_hbm(face_table.T)

    def rows(n):
        return jax.ShapeDtypeStruct((n, LANES), f32)

    half = 1024
    *pieces, rim = call(
        functools.partial(cells_kernel, planes),
        (mine_word, boxes, now),
        [SM, SM, HB],
        (rows(half // 2),) * 4 + (rows(holders * 128),),
        [
            pltpu.VMEM((2048, LANES), f32),
            pltpu.VMEM((32 * planes, LANES), f32),
            pltpu.VMEM((32 * planes, LANES), f32),
            pltpu.VMEM((holders * B, LANES), f32),
            pltpu.VMEM((holders, LANES, 2 * LANES), bf16),
            pltpu.VMEM((holders, LANES, 2 * LANES), bf16),
            pltpu.VMEM((holders, 144, LANES), bf16),
            pltpu.VMEM((holders, 144, LANES), bf16),
            pltpu.VMEM((B, (planes + 1) * LANES), bf16),
            pltpu.VMEM((B, (planes + 1) * LANES), bf16),
            pltpu.VMEM((B, (planes + 1) * LANES), bf16),
            pltpu.VMEM((B, (planes + 1) * LANES), bf16),
            pltpu.SemaphoreType.DMA,
        ],
    )
    pay, rim = call(
        functools.partial(pack_kernel, planes),
        (face_rows, rim),
        [HB, VM],
        (rows(domains * FACE_ROWS), pltpu.HBM((holders * 128, LANES), f32)),
        [
            pltpu.SMEM(face_rows.shape, jnp.int32),
            pltpu.SMEM((domains,), jnp.int32),
            pltpu.VMEM((domains * FACE_ROWS, LANES), f32),
            pltpu.SemaphoreType.DMA((3,)),
        ],
        spot=HB,
    )
    far = [swap(pieces[t], 2 * t) for t in range(1, 4)]
    arrived = lax.all_to_all(pay.reshape(-1, 1, LANES), "dom", 0, 0, tiled=True)

    near = [swap(x[half // 4 :], 1) for x in (pieces[0], *far)]

    order = (mine ^ jnp.arange(count, dtype=jnp.int32))[:, None] * planes
    order = (order + jnp.arange(planes, dtype=jnp.int32)).reshape(-1)
    depth_table = cosine(jnp.full((), total, jnp.int32), order[None, :], order[:, None])
    depth_table = jnp.concatenate([depth_table, depth_table], 1)
    mixed = call(
        functools.partial(depth_kernel, planes),
        (depth_table, pieces[0], *far, *near),
        [VM] * (2 + len(far) + len(near)),
        (rows(half),) * 2,
    )
    part = half // 4
    cuts = [slice(t * part, (t + 1) * part) for t in range(4)]
    back_near = [swap(mixed[1][cut], 1) for cut in cuts]
    back_far = [
        swap(jnp.concatenate([mixed[0][cuts[t]], back_near[t]], 0), 2 * t)
        for t in range(1, 4)
    ]

    later, _ = lax.optimization_barrier((boxes, mixed[0]))
    tables = call(
        tables_kernel,
        (later,),
        [SM],
        tuple(
            pltpu.HBM((holders, n, LANES), f32) for n in (B, B, 32, 2 * RIM)
        ),
        [
            pltpu.VMEM((holders, B, LANES), f32),
            pltpu.VMEM((holders, B, LANES), f32),
            pltpu.VMEM((holders, 32, LANES), f32),
            pltpu.VMEM((holders, 2 * RIM, LANES), f32),
            pltpu.SemaphoreType.DMA((4,)),
        ],
        spot=HB,
    )
    new = call(
        functools.partial(advance_kernel, planes, total),
        (mine_word, boxes, arrived.reshape(-1, LANES), in_hbm(rim), now, prev)
        + tuple(in_hbm(t) for t in tables),
        [SM] * 2 + [VM] + [HB] * 7,
        rows(2048),
        [
            pltpu.VMEM((holders * 128, LANES), f32),
            pltpu.VMEM((holders * 2 * RIM, LANES), f32),
            pltpu.VMEM((2048, LANES), f32),
            pltpu.VMEM((2048, LANES), f32),
            pltpu.VMEM((holders * 128, LANES), f32),
            pltpu.VMEM((holders, B, LANES), f32),
            pltpu.VMEM((holders, B, LANES), f32),
            pltpu.VMEM((holders, 32, LANES), f32),
            pltpu.VMEM((holders, 16, LANES), f32),
            pltpu.VMEM((domains, LANES), jnp.int32),
            pltpu.SMEM((domains, LANES), jnp.int32),
        ]
        + [
            pltpu.VMEM((32, LANES), f32),
            pltpu.VMEM((2 * RIM, planes * LANES), bf16),
            pltpu.VMEM((2 * RIM, planes * LANES), bf16),
        ]
        * 2
        + [pltpu.SemaphoreType.DMA((8,))],
    )
    pressure = call(
        functools.partial(join_kernel, planes),
        (mine_word, *[b.reshape(-1, 32, LANES) for b in (mixed[0], back_near[0], *back_far)]),
        [SM] + [VM] * (2 + len(back_far)),
        jax.ShapeDtypeStruct((planes, 256, LANES), f32),
        [pltpu.SemaphoreType.DMA((count,))],
        spot=HB,
    )
    pressure = untiles(pressure.reshape(-1, LANES), planes, holders)
    return untiles(new, planes, holders), pressure


def solution(mesh):
    placed = (P("height", "dom", None), P("height", "dom", None), P("dom", None), P("dom", None))
    return jax.shard_map(
        step,
        mesh=mesh,
        in_specs=placed,
        out_specs=(P("height", "dom", None), P("height", "dom", None)),
        check_vma=False,
    )
```
